512 devices in a mesh: row: 32 (over z_lo, x, core), col: 16 (over y, z_hi).
Axes of the slice: x: 4, y: 4, z: 16 (z_hi: 4, z_lo: 4; z = z_hi * 4 + z_lo), core: 2. Of those that a mesh axis runs over, the one named last changes fastest.
Arguments:
- features: bfloat16 [65536, 512], P(('col', 'row')), may hold values from -6 to 6
- tile_values: bfloat16 [32, 16, 6, 256, 256], P('row', 'col'), may hold values from -0.109375 to 0.109375
- tile_index: int32 [32, 16, 6], P('row', 'col'), may hold values from 0 to 127, as said below
- tile_count: int32 [32, 16], P('row', 'col'), may hold values from 1 to 6, as said below
- weight: bfloat16 [512, 512], replicated, may hold values from -0.25 to 0.25
- cotangent: bfloat16 [65536, 512], P(('row', 'col')), may hold values from -6 to 6
Outputs:
- output: bfloat16 [65536, 512], P(('row', 'col'))
- weight_grad: float32 [512, 512], replicated
The draws below stay inside these ranges and needn't reach their ends.
Inputs may be any that keep to these rules, and one draw needn't show every extreme that they name: `tile_index`: on each device the 6 slots hold different tile numbers. `tile_count`: some device has all 6 slots live.
All inputs are finite; a program needn't handle non-finite values.
Results may differ from the reference program's by a relative error of at most 0.024.
Values may be sent and summed in bfloat16 or wider, within the bound.
A program may use at most 64 MiB of HBM per device.

```python
import math
import jax
import jax.numpy as jnp
from jax import lax

F = 512
BLK = 256
RBG = 8
KMAX = 6
CBG = 16
V = 65536
N_ROW = 32
N_COL = 16


def draw_tile_index(key, part):
    subkeys = jax.random.split(jax.random.fold_in(key, 11), N_ROW * N_COL)

    def one_device(subkey):
        return jax.random.permutation(subkey, RBG * CBG)[:KMAX]
    return jax.vmap(one_device)(subkeys).reshape(N_ROW, N_COL, KMAX).astype(jnp.int32)


def draw_tile_count(key, part):
    first = jax.random.randint(jax.random.fold_in(key, 21), (N_ROW, N_COL), 1, KMAX + 1)
    second = jax.random.randint(jax.random.fold_in(key, 22), (N_ROW, N_COL), 1, KMAX + 1)
    counts = jnp.minimum(first, second)
    chosen = jax.random.randint(jax.random.fold_in(key, 23), (), 0, N_ROW * N_COL)
    flat_ids = jnp.arange(N_ROW * N_COL).reshape(N_ROW, N_COL)
    return jnp.where(flat_ids == chosen, KMAX, counts).astype(jnp.int32)


def levels(key, extent, cuts, smallest, top_value):
    loudness, own = 1.0, jax.random.fold_in(key, 6)
    for position, parts in cuts:
        heights = jnp.exp(jax.random.uniform(jax.random.fold_in(own, position), (parts,), jnp.float32, smallest / len(cuts), top_value / len(cuts)))
        loudness = loudness * jnp.repeat(heights, extent[position] // parts).reshape([-1 if axis == position else 1 for axis in range(len(extent))])
    return loudness


def scatter_about(stream_key, extent, spread, bound, pieces=(), kind=jnp.bfloat16):
    array = spread * jax.random.normal(stream_key, extent, jnp.float32)
    if pieces:
        array = array * levels(stream_key, extent, pieces, -0.22, 0.18)
    return jnp.clip(array, -bound, bound).astype(kind)


def setup_inputs(seed: int = 0) -> dict:
    keys = jax.random.split(jax.random.key(seed), 7)
    features = scatter_about(keys[0], (V, F), 1.0, 6.0, ((0, 512),))
    tile_values = scatter_about(keys[1], (N_ROW, N_COL, KMAX, BLK, BLK), (BLK * KMAX * N_ROW // CBG) ** -0.5, 0.109375, ((0, 32), (1, 16)))
    tile_index = draw_tile_index(jax.random.fold_in(keys[6], 71), 0)
    tile_count = draw_tile_count(jax.random.fold_in(keys[6], 71), 0)
    weight = scatter_about(keys[4], (F, F), F ** -0.5, 0.25)
    cotangent = scatter_about(keys[5], (V, F), 1.0, 6.0, ((0, 512),))
    return {"features": features, "tile_values": tile_values, "tile_index": tile_index, "tile_count": tile_count, "weight": weight, "cotangent": cotangent}


def reference(features, tile_values, tile_index, tile_count, weight, cotangent):
    blocks = features.reshape(-1, BLK, F)

    def one_group(group):
        tile_vals = tile_values[group].astype(jnp.float32)
        tile_ids = tile_index[group]
        live_count = tile_count[group]
        row_slot = tile_ids // CBG
        col_slot = tile_ids % CBG
        global_col = jnp.arange(N_COL, dtype=jnp.int32)[:, None] * CBG + col_slot
        picked = blocks[global_col].astype(jnp.float32)
        is_live = jnp.arange(KMAX, dtype=jnp.int32)[None, :] < live_count[:, None]
        placing = ((row_slot[:, :, None] == jnp.arange(RBG, dtype=jnp.int32)[None, None, :]) & is_live[:, :, None]).astype(jnp.float32)
        products = jnp.einsum('ckab,ckbf->ckaf', tile_vals, picked)
        partial_value = jnp.einsum('ckr,ckaf->craf', placing, products).astype(jnp.bfloat16)
        partial_value = lax.optimization_barrier(partial_value)
        return lax.optimization_barrier(jnp.sum(partial_value.astype(jnp.float32), axis=0))
    summed = lax.map(one_group, jnp.arange(N_ROW, dtype=jnp.int32))
    aggregated = summed.reshape(-1, F).astype(jnp.bfloat16)
    preact = jnp.dot(aggregated, weight, preferred_element_type=jnp.float32)
    output = jnp.where(preact > 0, preact, jnp.expm1(jnp.minimum(preact, 0.0))).astype(jnp.bfloat16)
    slope = jnp.where(preact > 0, 1.0, jnp.exp(jnp.minimum(preact, 0.0)))
    grad_pre = (cotangent.astype(jnp.float32) * slope).astype(jnp.bfloat16)
    weight_grad = jnp.dot(aggregated.T, grad_pre, preferred_element_type=jnp.float32) * (1.0 / math.sqrt(V))
    return (output, weight_grad)
```

```python
import functools
import math

import jax
import jax.numpy as jnp
from jax import lax
from jax.experimental import pallas as pl
from jax.experimental.pallas import tpu as pltpu
from jax.sharding import PartitionSpec as P

F = 512
BLK = 256
RBG = 8
KMAX = 6
CBG = 16
OWN = 128
NC = 2
FC = F // NC
MESH = pl.DeviceIdType.MESH
BF16 = jnp.bfloat16
F32 = jnp.float32


def remote(src, dst, send, recv, device):
    copy = pltpu.make_async_remote_copy(
        src_ref=src, dst_ref=dst, send_sem=send, recv_sem=recv, device_id=device, device_id_type=MESH
    )
    copy.start()


def arrived(view, sem):
    pltpu.make_async_copy(view, view, sem).wait()


def kernel(
    scale,
    features, tiles, index, count, weight, cotangent,
    output, weight_grad,
    got, tile, wts, cot, sums, part, part_l, part_r, quar, quar_l, quar_r, agg,
    grad, core_out, core_in, half, xy_in, z_out, z_in, z_all, full,
    s_local, s_z, s_l, s_r, s_top, s_bot, s_sib, s_send, s_sibsend, s_y, s_q, s_gsend, s_grecv,
):
    row, col = lax.axis_index("row"), lax.axis_index("col")
    core = lax.rem(row, 2)
    block = lax.div(row, 2)
    x, z_lo = lax.rem(block, 4), lax.div(block, 4)
    y, z_hi = lax.div(col, 4), lax.rem(col, 4)
    other = 1 - core
    chip_xy = x * 4 + y
    z = z_hi * 4 + z_lo

    def at(x_=x, y_=y, z_lo_=z_lo, z_hi_=z_hi, core_=core):
        return ((z_lo_ * 4 + x_) * 2 + core_, y_ * 4 + z_hi_)

    def at_xy(i):
        return at(x_=lax.div(i, 4), y_=lax.rem(i, 4))

    def at_z(i):
        return at(z_lo_=lax.rem(i, 4), z_hi_=lax.div(i, 4))

    sibling = at(core_=other)
    x_right, x_left = at(x_=lax.rem(x + 1, 4)), at(x_=lax.rem(x + 3, 4))

    barrier = pltpu.get_barrier_semaphore()
    pl.semaphore_signal(barrier, inc=1, device_id=sibling, device_id_type=MESH)
    for d in range(1, 16):
        pl.semaphore_signal(barrier, inc=1, device_id=at_xy(lax.rem(chip_xy + d, 16)), device_id_type=MESH)
        pl.semaphore_signal(barrier, inc=1, device_id=at_z(lax.rem(z + d, 16)), device_id_type=MESH)

    own = [
        pltpu.make_async_copy(
            features.at[pl.ds(t * 64, 64), pl.ds(j * FC, FC)],
            got[j].at[block, 2 * core + t],
            s_local.at[2 * j + t],
        )
        for j in range(NC) for t in range(2)
    ]
    later = [
        pltpu.make_async_copy(tiles.at[0, 0], tile, s_local.at[2 * NC]),
        pltpu.make_async_copy(weight, wts, s_local.at[2 * NC + 1]),
        pltpu.make_async_copy(cotangent, cot, s_local.at[2 * NC + 2]),
    ]
    for copy in own + later:
        copy.start()

    slot_row = []
    slot_col = []
    live = count[0, 0]
    for k in range(KMAX):
        number = index[0, 0, k]
        slot_row.append(jnp.where(k < live, lax.div(number, CBG), RBG))
        slot_col.append(lax.rem(number, CBG))
    rank = []
    for k in range(KMAX):
        before = jnp.int32(0)
        for m in range(KMAX):
            if m != k:
                ahead = slot_row[m] <= slot_row[k] if m < k else slot_row[m] < slot_row[k]
                before = before + jnp.where(ahead, 1, 0)
        rank.append(before)
    take, take_row, take_col = [], [], []
    for s in range(KMAX):
        picked = [jnp.where(rank[k] == s, 1, 0) for k in range(KMAX)]
        take.append(sum(k * picked[k] for k in range(KMAX)))
        take_row.append(sum(slot_row[k] * picked[k] for k in range(KMAX)))
        take_col.append(sum(slot_col[k] * picked[k] for k in range(KMAX)))
    last = []
    for r in range(RBG):
        upto = sum(jnp.where(slot_row[k] <= r, 1, 0) for k in range(KMAX))
        here = sum(jnp.where(slot_row[k] == r, 1, 0) for k in range(KMAX))
        last.append(jnp.where(here > 0, upto - 1, KMAX))

    sums[KMAX] = jnp.zeros((BLK, FC), BF16)
    for copy in own:
        copy.wait()
    pl.semaphore_wait(barrier, 31)

    def shard(j, p):
        return got[j].at[p, pl.ds(2 * core, 2)]

    def give(j, p, sems, device):
        remote(shard(j, p), shard(j, p), s_send.at[j], sems, device)

    def give_half(j, p, t, sem, device):
        piece = got[j].at[p, 2 * core + t]
        remote(piece, piece, s_send.at[j], sem, device)

    def give_sibling(j, p):
        remote(shard(j, p), shard(j, p), s_sibsend.at[j], s_sib.at[j], sibling)

    def spread(j, d):
        p = lax.rem(z_lo + d, 4) * 4 + x
        give(j, p, s_l.at[j, d], x_right)
        give(j, p, s_r.at[j, d], x_left)
        give_sibling(j, p)

    def gather_start(j):
        for d in range(1, 4):
            give(j, block, s_z.at[j, 4 - d], at(z_lo_=lax.rem(z_lo + d, 4)))
        spread(j, 0)

    def gather_z(j):
        for d in range(1, 4):
            arrived(shard(j, lax.rem(z_lo + d, 4) * 4 + x), s_z.at[j, d])
            spread(j, d)

    def gather_x(j):
        for d in range(4):
            line = lax.rem(z_lo + d, 4) * 4
            p_l, p_r = line + lax.rem(x + 3, 4), line + lax.rem(x + 1, 4)
            arrived(shard(j, p_l), s_l.at[j, d])
            give_half(j, p_l, 0, s_top.at[j, d], x_right)
            give_sibling(j, p_l)
            arrived(shard(j, p_r), s_r.at[j, d])
            give_half(j, p_r, 1, s_bot.at[j, d], x_left)
            give_sibling(j, p_r)

    def gather_end(j):
        for d in range(4):
            p = lax.rem(z_lo + d, 4) * 4 + lax.rem(x + 2, 4)
            arrived(got[j].at[p, 2 * core], s_top.at[j, d])
            arrived(got[j].at[p, 2 * core + 1], s_bot.at[j, d])
            give_sibling(j, p)
        arrived(got[j].at[:, pl.ds(2 * other, 2)], s_sib.at[j])

    def multiply(j):
        for s in range(KMAX):
            features_block = got[j][take_col[s]].reshape(BLK, FC)
            product = jnp.dot(tile[take[s]], features_block, preferred_element_type=F32)
            if s:
                product = product + jnp.where(take_row[s] == take_row[s - 1], running, 0.0)
            running = product
            sums[s] = running.astype(BF16)
        for r in range(RBG):
            part[j, r] = sums[last[r]]

    def ring_start(j, buf, from_l, from_r, me, right, left, sems):
        nxt, opp, prv = lax.rem(me + 1, 4), lax.rem(me + 2, 4), lax.rem(me + 3, 4)
        remote(buf.at[j, 2 * opp], from_l.at[j, 0], sems.at[j, 0], sems.at[j, 1], right)
        remote(buf.at[j, 2 * opp + 1], from_r.at[j, 0], sems.at[j, 0], sems.at[j, 2], left)
        remote(buf.at[j, 2 * nxt + 1], from_l.at[j, 2], sems.at[j, 0], sems.at[j, 3], right)
        remote(buf.at[j, 2 * prv], from_r.at[j, 1], sems.at[j, 0], sems.at[j, 4], left)

    def ring_turn(j, buf, from_l, from_r, me, right, left, sems):
        nxt, prv = lax.rem(me + 1, 4), lax.rem(me + 3, 4)
        arrived(from_l.at[j, 0], sems.at[j, 1])
        buf[j, 2 * nxt] = (buf[j, 2 * nxt].astype(F32) + from_l[j, 0].astype(F32)).astype(BF16)
        remote(buf.at[j, 2 * nxt], from_l.at[j, 1], sems.at[j, 0], sems.at[j, 3], right)
        arrived(from_r.at[j, 0], sems.at[j, 2])
        buf[j, 2 * prv + 1] = (buf[j, 2 * prv + 1].astype(F32) + from_r[j, 0].astype(F32)).astype(BF16)
        remote(buf.at[j, 2 * prv + 1], from_r.at[j, 2], sems.at[j, 0], sems.at[j, 4], left)

    def ring_end(j, buf, from_l, from_r, me, sems):
        arrived(from_l.at[j, pl.ds(1, 2)], sems.at[j, 3])
        arrived(from_r.at[j, pl.ds(1, 2)], sems.at[j, 4])
        return [
            buf[j, 2 * me + t].astype(F32) + from_l[j, 1 + t].astype(F32) + from_r[j, 1 + t].astype(F32)
            for t in range(2)
        ]

    ring_y = (part, part_l, part_r)
    ring_q = (quar, quar_l, quar_r)
    dev_y = (y, at(y_=lax.rem(y + 1, 4)), at(y_=lax.rem(y + 3, 4)))
    dev_q = (z_hi, at(z_hi_=lax.rem(z_hi + 1, 4)), at(z_hi_=lax.rem(z_hi + 3, 4)))

    def y_start(j):
        ring_start(j, *ring_y, *dev_y, s_y)

    def y_turn(j):
        ring_turn(j, *ring_y, *dev_y, s_y)

    def y_end(j):
        for t, value in enumerate(ring_end(j, *ring_y, y, s_y)):
            quar[j, pl.ds(4 * t, 4)] = value.astype(BF16).reshape(4, 64, FC)
        ring_start(j, *ring_q, *dev_q, s_q)

    def q_turn(j):
        ring_turn(j, *ring_q, *dev_q, s_q)

    def q_end(j):
        for t, value in enumerate(ring_end(j, *ring_q, z_hi, s_q)):
            agg[pl.ds(64 * t, 64), pl.ds(j * FC, FC)] = value.astype(BF16)

    for j in range(NC):
        gather_start(j)
    later[0].wait()
    for j in range(NC):
        gather_z(j)
        if j:
            y_turn(j - 1)
        gather_x(j)
        if j:
            y_end(j - 1)
        gather_end(j)
        multiply(j)
        y_start(j)
        if j:
            q_turn(j - 1)
    y_turn(NC - 1)
    if NC > 1:
        q_end(NC - 2)
    y_end(NC - 1)
    q_turn(NC - 1)
    q_end(NC - 1)

    later[1].wait()
    later[2].wait()
    aggregated = agg[...]
    preact = jnp.dot(aggregated, wts[...], preferred_element_type=F32)
    low = jnp.minimum(preact, 0.0)
    slope = jnp.exp(low)
    near = low * (1.0 + low * (0.5 + low * (1.0 / 6 + low * (1.0 / 24))))
    output[...] = jnp.where(preact > 0, preact, jnp.where(low > -0.03125, near, slope - 1.0)).astype(BF16)
    grad_pre = (cot[...].astype(F32) * slope).astype(BF16)
    grad[...] = scale * lax.dot_general(
        aggregated, grad_pre, (((0,), (0,)), ((), ())), preferred_element_type=F32
    )

    @pl.loop(0, 16)
    def _(i):
        for g in range(4):
            core_out[i, g] = grad[pl.ds(other * 256 + i * 16, 16), pl.ds(g * 128, 128)].astype(BF16)

    remote(core_out, core_in, s_gsend.at[0], s_grecv.at[0], sibling)
    arrived(core_in, s_grecv.at[0])

    @pl.loop(0, 16)
    def _(i):
        for g in range(4):
            mine = grad[pl.ds(core * 256 + i * 16, 16), pl.ds(g * 128, 128)]
            half[i, g] = (mine + core_in[i, g].astype(F32)).astype(BF16)

    @pl.loop(1, 16)
    def _(d):
        i = lax.rem(chip_xy + d, 16)
        remote(half.at[i], xy_in.at[chip_xy], s_gsend.at[1], s_grecv.at[1], at_xy(i))

    xy_in[chip_xy] = half[chip_xy]
    arrived(xy_in.at[pl.ds(0, 15)], s_grecv.at[1])
    total = xy_in[0].astype(F32)
    for i in range(1, 16):
        total = total + xy_in[i].astype(F32)
    z_out[...] = total.astype(BF16)

    @pl.loop(1, 16)
    def _(d):
        i = lax.rem(z + d, 16)
        remote(z_out.at[lax.rem(i, 4)], z_in.at[z], s_gsend.at[2], s_grecv.at[2], at_z(i))

    z_in[z] = z_out[z_lo]
    arrived(z_in.at[pl.ds(0, 15)], s_grecv.at[2])
    total = z_in[0].astype(F32)
    for i in range(1, 16):
        total = total + z_in[i].astype(F32)
    z_all[z_lo] = total.astype(BF16)
    for d in range(1, 4):
        remote(z_all.at[z_lo], z_all.at[z_lo], s_gsend.at[3], s_grecv.at[3], at(z_lo_=lax.rem(z_lo + d, 4)))
    arrived(z_all.at[pl.ds(0, 3)], s_grecv.at[3])
    full[core, chip_xy] = z_all[...]

    @pl.loop(1, 16)
    def _(d):
        i = lax.rem(chip_xy + d, 16)
        piece = full.at[core, chip_xy]
        remote(piece, piece, s_gsend.at[4], s_grecv.at[4], at_xy(i))

    arrived(full.at[core, pl.ds(0, 15)], s_grecv.at[4])
    remote(full.at[core], full.at[core], s_gsend.at[5], s_grecv.at[5], sibling)
    arrived(full.at[other], s_grecv.at[5])
    for k in range(2):
        @pl.loop(0, 16)
        def _(i):
            for g in range(4):
                weight_grad[pl.ds(k * 256 + i * 16, 16), pl.ds(g * 128, 128)] = full[k, i, g].astype(F32)

    for j in range(NC):
        arrived(got[j].at[pl.ds(0, 15), pl.ds(0, 2)], s_send.at[j])
        arrived(got[j].at[:, pl.ds(0, 2)], s_sibsend.at[j])
        arrived(part.at[j, pl.ds(0, 6)], s_y.at[j, 0])
        arrived(quar.at[j, pl.ds(0, 6)], s_q.at[j, 0])
    arrived(core_out, s_gsend.at[0])
    arrived(half.at[pl.ds(0, 15)], s_gsend.at[1])
    arrived(z_in.at[pl.ds(0, 15)], s_gsend.at[2])
    arrived(z_all.at[pl.ds(0, 3)], s_gsend.at[3])
    arrived(full.at[0, pl.ds(0, 15)], s_gsend.at[4])
    arrived(full.at[0], s_gsend.at[5])


def solution(mesh):
    vmem, smem, hbm = pltpu.VMEM, pltpu.SMEM, pl.ANY
    dma = pltpu.SemaphoreType.DMA

    def local(*operands):
        scale = 1.0 / math.sqrt(RBG * BLK * mesh.shape["row"])
        return pl.pallas_call(
            functools.partial(kernel, scale),
            out_shape=(
                jax.ShapeDtypeStruct((OWN, F), BF16),
                jax.ShapeDtypeStruct((F, F), F32),
            ),
            in_specs=[pl.BlockSpec(memory_space=s) for s in (hbm, hbm, smem, smem, hbm, hbm)],
            out_specs=[pl.BlockSpec(memory_space=vmem)] * 2,
            scratch_shapes=[
                [vmem((CBG, 4, 64, FC), BF16)] * NC,
                vmem((KMAX, BLK, BLK), BF16),
                vmem((F, F), BF16),
                vmem((OWN, F), BF16),
                vmem((KMAX + 1, BLK, FC), BF16),
                vmem((NC, RBG, BLK, FC), BF16),
                vmem((NC, 3, BLK, FC), BF16),
                vmem((NC, 3, BLK, FC), BF16),
                vmem((NC, 8, 64, FC), BF16),
                vmem((NC, 3, 64, FC), BF16),
                vmem((NC, 3, 64, FC), BF16),
                vmem((OWN, F), BF16),
                vmem((F, F), F32),
                vmem((16, 4, 16, 128), BF16),
                vmem((16, 4, 16, 128), BF16),
                vmem((16, 4, 16, 128), BF16),
                vmem((16, 4, 16, 128), BF16),
                vmem((4, 16, 128), BF16),
                vmem((16, 16, 128), BF16),
                vmem((4, 16, 128), BF16),
                vmem((2, 16, 4, 16, 128), BF16),
                dma((2 * NC + 3,)),
                dma((NC, 4)), dma((NC, 4)), dma((NC, 4)), dma((NC, 4)), dma((NC, 4)),
                dma((NC,)), dma((NC,)), dma((NC,)),
                dma((NC, 5)), dma((NC, 5)),
                dma((6,)), dma((6,)),
            ],
            compiler_params=pltpu.CompilerParams(
                collective_id=0, has_side_effects=True, vmem_limit_bytes=48 << 20
            ),
        )(*operands)

    placed = (
        P(("col", "row"), None),
        P("row", "col", None, None, None),
        P("row", "col", None),
        P("row", "col"),
        P(),
        P(("row", "col"), None),
    )
    return jax.shard_map(
        local, mesh=mesh, in_specs=placed, out_specs=(P(("row", "col"), None), P()), check_vma=False
    )
```

```python
import functools
import math

import jax
import jax.numpy as jnp
from jax import lax
from jax.experimental import pallas as pl
from jax.experimental.pallas import tpu as pltpu
from jax.sharding import PartitionSpec as P

F = 512
HALF = F // 2
BLK = 256
RBG = 8
KMAX = 6
CBG = 16
OWN = 128
NC = 2
FC = HALF // NC
MESH = pl.DeviceIdType.MESH
BF16 = jnp.bfloat16
F32 = jnp.float32


def remote(src, dst, send, recv, device):
    copy = pltpu.make_async_remote_copy(
        src_ref=src, dst_ref=dst, send_sem=send, recv_sem=recv, device_id=device, device_id_type=MESH
    )
    copy.start()


def arrived(view, sem):
    pltpu.make_async_copy(view, view, sem).wait()


def plan_of(index, count):
    slot_row, slot_col = [], []
    for k in range(KMAX):
        number = index[0, 0, k]
        slot_row.append(jnp.where(k < count[0, 0], lax.div(number, CBG), RBG))
        slot_col.append(lax.rem(number, CBG))
    rank = []
    for k in range(KMAX):
        before = jnp.int32(0)
        for m in range(KMAX):
            if m != k:
                ahead = slot_row[m] <= slot_row[k] if m < k else slot_row[m] < slot_row[k]
                before = before + jnp.where(ahead, 1, 0)
        rank.append(before)
    take, take_row, take_col = [], [], []
    for s in range(KMAX):
        picked = [jnp.where(rank[k] == s, 1, 0) for k in range(KMAX)]
        take.append(sum(k * picked[k] for k in range(KMAX)))
        take_row.append(sum(slot_row[k] * picked[k] for k in range(KMAX)))
        take_col.append(sum(slot_col[k] * picked[k] for k in range(KMAX)))
    goes_on = [jnp.int32(0)] + [
        jnp.where(take_row[s] == take_row[s - 1], 1, 0) for s in range(1, KMAX)
    ]
    last = []
    for r in range(RBG):
        upto = sum(jnp.where(slot_row[k] <= r, 1, 0) for k in range(KMAX))
        here = sum(jnp.where(slot_row[k] == r, 1, 0) for k in range(KMAX))
        last.append(jnp.where(here > 0, upto - 1, KMAX))
    return take + take_col + goes_on + last


def kernel(
    scale,
    features, tiles, index, count, weight, cotangent,
    output, weight_grad,
    staged, swap, got, tile, wts, cot, plan_out, plan_in, plan_s, sums, part, part_l, part_r, quar, quar_l, quar_r, res, cross,
    mine, core_out, core_in, half, xy_in, z_out, z_in, z_all, full,
    s_local, s_plan, s_swap, s_tile, s_z, s_l, s_r, s_top, s_bot, s_send, s_y, s_q, s_cross, s_gsend, s_grecv, s_far,
):
    row, col = lax.axis_index("row"), lax.axis_index("col")
    core = lax.rem(row, 2)
    block = lax.div(row, 2)
    x, z_lo = lax.rem(block, 4), lax.div(block, 4)
    y, z_hi = lax.div(col, 4), lax.rem(col, 4)
    other = 1 - core
    chip_xy = x * 4 + y
    z = z_hi * 4 + z_lo

    def at(x_=x, y_=y, z_lo_=z_lo, z_hi_=z_hi, core_=core):
        return ((z_lo_ * 4 + x_) * 2 + core_, y_ * 4 + z_hi_)

    def at_xy(i):
        return at(x_=lax.div(i, 4), y_=lax.rem(i, 4))

    def at_z(i):
        i = lax.rem(i, 16)
        return at(z_lo_=lax.rem(i, 4), z_hi_=lax.div(i, 4))

    def turn(i, d):
        return lax.rem(i + d, 4)

    sibling = at(core_=other)
    x_right, x_left = at(x_=turn(x, 1)), at(x_=turn(x, 3))
    y_right, y_left = at(y_=turn(y, 1)), at(y_=turn(y, 3))

    barrier = pltpu.get_barrier_semaphore()
    near = [sibling, x_right, x_left, y_right, y_left] + [at_z(z + 16 + d) for d in (1, -1, 2, -2, 3, -3)]
    for device in near:
        pl.semaphore_signal(barrier, inc=1, device_id=device, device_id_type=MESH)

    own = [pltpu.make_async_copy(features, staged, s_local.at[0])]
    later = [
        pltpu.make_async_copy(tiles.at[0, 0], tile[0], s_local.at[NC]),
        pltpu.make_async_copy(weight, wts, s_local.at[NC + 1]),
        pltpu.make_async_copy(cotangent, cot, s_local.at[NC + 2]),
    ]
    own[0].start()

    plan = plan_of(index, count)
    lane = lax.broadcasted_iota(jnp.int32, (8, 128), 1)
    table = jnp.zeros((8, 128), jnp.int32)
    for i, entry in enumerate(plan):
        table = jnp.where(lane == i, entry, table)
    plan_out[...] = table
    sums[KMAX] = jnp.zeros((BLK, FC), BF16)

    def columns(whose, j):
        return staged[:, pl.ds(pl.multiple_of(whose * HALF + j * FC, FC), FC)]

    own[0].wait()
    for j in range(NC):
        swap[j] = columns(other, j)
        got[j][block, core] = columns(core, j)
    pl.semaphore_wait(barrier, 11)
    pl.semaphore_signal(s_far.at[0], inc=1, device_id=at_z(z + 13), device_id_type=MESH)
    pl.semaphore_signal(s_far.at[1], inc=1, device_id=at_z(z + 3), device_id_type=MESH)

    for j in range(NC):
        remote(swap.at[j], got[j].at[block, core], s_plan.at[2 + j], s_swap.at[j], sibling)
    remote(plan_out, plan_in, s_plan.at[0], s_plan.at[1], sibling)

    def give(j, p, sem, device):
        remote(got[j].at[p], got[j].at[p], s_send.at[j], sem, device)

    def give_half(j, p, t, sem, device):
        remote(got[j].at[p, t], got[j].at[p, t], s_send.at[j], sem, device)

    def spread(j, d):
        p = turn(z_lo, d) * 4 + x
        give(j, p, s_l.at[j, d], x_right)
        give(j, p, s_r.at[j, d], x_left)

    def gather_start(j):
        arrived(got[j].at[block, other], s_swap.at[j])
        for d in (1, 3, 2):
            give(j, block, s_z.at[j, 4 - d], at(z_lo_=turn(z_lo, d)))
        spread(j, 0)

    def gather_z(j):
        for d in range(1, 4):
            arrived(got[j].at[turn(z_lo, d) * 4 + x], s_z.at[j, d])
            spread(j, d)

    def gather_x(j, part=range(4)):
        for d in part:
            line = turn(z_lo, d) * 4
            p_l, p_r = line + turn(x, 3), line + turn(x, 1)
            arrived(got[j].at[p_l], s_l.at[j, d])
            give_half(j, p_l, 0, s_top.at[j, d], x_right)
            arrived(got[j].at[p_r], s_r.at[j, d])
            give_half(j, p_r, 1, s_bot.at[j, d], x_left)

    def gather_end(j):
        for d in range(4):
            p = turn(z_lo, d) * 4 + turn(x, 2)
            arrived(got[j].at[p, 0], s_top.at[j, d])
            arrived(got[j].at[p, 1], s_bot.at[j, d])

    def multiply(u):
        j = u // 2
        entry = (lambda i: plan_s[0, i]) if u % 2 else (lambda i: plan[i])
        for s in range(KMAX):
            features_block = got[j][entry(KMAX + s)].reshape(BLK, FC)
            product = jnp.dot(tile[u % 2][entry(s)], features_block, preferred_element_type=F32)
            if s:
                product = product + jnp.where(entry(2 * KMAX + s) == 1, running, 0.0)
            running = product
            sums[s] = running.astype(BF16)
        for r in range(RBG):
            part[u, r] = sums[entry(3 * KMAX + r)]

    def ring_start(j, buf, from_l, from_r, me, right, left, sems):
        nxt, opp, prv = turn(me, 1), turn(me, 2), turn(me, 3)
        remote(buf.at[j, 2 * opp], from_l.at[j, 0], sems.at[j, 0], sems.at[j, 1], right)
        remote(buf.at[j, 2 * opp + 1], from_r.at[j, 0], sems.at[j, 0], sems.at[j, 2], left)
        remote(buf.at[j, 2 * nxt + 1], from_l.at[j, 2], sems.at[j, 0], sems.at[j, 3], right)
        remote(buf.at[j, 2 * prv], from_r.at[j, 1], sems.at[j, 0], sems.at[j, 4], left)

    def ring_turn(j, buf, from_l, from_r, me, right, left, sems):
        nxt, prv = turn(me, 1), turn(me, 3)
        arrived(from_l.at[j, 0], sems.at[j, 1])
        buf[j, 2 * nxt] = (buf[j, 2 * nxt].astype(F32) + from_l[j, 0].astype(F32)).astype(BF16)
        remote(buf.at[j, 2 * nxt], from_l.at[j, 1], sems.at[j, 0], sems.at[j, 3], right)
        arrived(from_r.at[j, 0], sems.at[j, 2])
        buf[j, 2 * prv + 1] = (buf[j, 2 * prv + 1].astype(F32) + from_r[j, 0].astype(F32)).astype(BF16)
        remote(buf.at[j, 2 * prv + 1], from_r.at[j, 2], sems.at[j, 0], sems.at[j, 4], left)

    def ring_end(j, buf, from_l, from_r, me, sems):
        arrived(from_l.at[j, pl.ds(1, 2)], sems.at[j, 3])
        arrived(from_r.at[j, pl.ds(1, 2)], sems.at[j, 4])
        return [
            (buf[j, 2 * me + t].astype(F32) + from_l[j, 1 + t].astype(F32) + from_r[j, 1 + t].astype(F32)).astype(BF16)
            for t in range(2)
        ]

    ring_y = (part, part_l, part_r)
    ring_q = (quar, quar_l, quar_r)
    dev_y = (y, y_right, y_left)
    dev_q = (z_hi, at(z_hi_=turn(z_hi, 1)), at(z_hi_=turn(z_hi, 3)))

    def y_start(j):
        ring_start(j, *ring_y, *dev_y, s_y)

    def y_turn(j):
        ring_turn(j, *ring_y, *dev_y, s_y)

    def y_end(j):
        for t, value in enumerate(ring_end(j, *ring_y, y, s_y)):
            for q in range(4):
                quar[j, 4 * t + q] = value[q * 64:(q + 1) * 64]
        ring_start(j, *ring_q, *dev_q, s_q)

    def q_turn(j):
        ring_turn(j, *ring_q, *dev_q, s_q)

    def q_end(u):
        for t, value in enumerate(ring_end(u, *ring_q, z_hi, s_q)):
            res[u, pl.ds(64 * t, 64)] = value
        if u % 2:
            remote(res.at[u], cross.at[u // 2], s_cross.at[u // 2, 0], s_cross.at[u // 2, 1], sibling)

    gather_start(0)
    for copy in later:
        copy.start()
    later[0].wait()
    remote(tile[0], tile[1], s_tile.at[0], s_tile.at[1], sibling)
    arrived(plan_in, s_plan.at[1])
    to_scalars = pltpu.make_async_copy(plan_in, plan_s, s_local.at[NC + 3])
    to_scalars.start()
    gather_z(0)
    gather_start(1)
    gather_x(0)
    gather_z(1)
    gather_end(0)
    multiply(0)
    y_start(0)
    to_scalars.wait()
    arrived(tile[1], s_tile.at[1])
    multiply(1)
    y_start(1)
    gather_x(1, (0, 1))
    y_turn(0)
    gather_x(1, (2, 3))
    y_turn(1)
    pl.semaphore_wait(s_far.at[0], 1)
    pl.semaphore_wait(s_far.at[1], 1)
    y_end(0)
    gather_end(1)
    multiply(3)
    y_start(3)
    y_end(1)
    multiply(2)
    y_start(2)
    q_turn(0)
    y_turn(3)
    q_turn(1)
    q_end(0)
    y_turn(2)
    y_end(3)
    q_end(1)
    y_end(2)
    q_turn(3)
    q_turn(2)
    q_end(3)
    q_end(2)

    later[1].wait()
    later[2].wait()

    def rows_of(whose, j):
        return pl.ds(pl.multiple_of(whose * HALF + j * FC, FC), FC)

    kept = [res[2 * j] for j in range(NC)]
    preact = sum(jnp.dot(kept[j], wts[rows_of(core, j)], preferred_element_type=F32) for j in range(NC))
    for j in range(NC):
        arrived(cross.at[j], s_cross.at[j, 1])
    swapped = [cross[j] for j in range(NC)]
    preact = preact + sum(
        jnp.dot(swapped[j], wts[rows_of(other, j)], preferred_element_type=F32) for j in range(NC)
    )
    low = jnp.minimum(preact, 0.0)
    slope = jnp.exp(low)
    near = low * (1.0 + low * (0.5 + low * (1.0 / 6 + low * (1.0 / 24))))
    output[...] = jnp.where(preact > 0, preact, jnp.where(low > -0.03125, near, slope - 1.0)).astype(BF16)
    grad_pre = (cot[...].astype(F32) * slope).astype(BF16)

    def term(aggregated):
        return scale * lax.dot_general(
            aggregated, grad_pre, (((0,), (0,)), ((), ())), preferred_element_type=F32
        )

    span = FC // 16
    for j in range(NC):
        value = term(swapped[j]).astype(BF16)
        for g in range(4):
            core_out[pl.ds(j * span, span), g] = value[:, g * 128:(g + 1) * 128].reshape(span, 16, 128)
    remote(core_out, core_in, s_gsend.at[0], s_grecv.at[0], sibling)
    for j in range(NC):
        value = term(kept[j])
        for g in range(4):
            mine[pl.ds(j * span, span), g] = value[:, g * 128:(g + 1) * 128].reshape(span, 16, 128)
    arrived(core_in, s_grecv.at[0])
    half[...] = (mine[...] + core_in[...].astype(F32)).astype(BF16)

    for d in range(1, 16):
        i = lax.rem(chip_xy + d, 16)
        remote(half.at[i], xy_in.at[chip_xy], s_gsend.at[1], s_grecv.at[1], at_xy(i))
    xy_in[chip_xy] = half[chip_xy]
    arrived(xy_in.at[pl.ds(0, 15)], s_grecv.at[1])
    total = xy_in[0].astype(F32)
    for i in range(1, 16):
        total = total + xy_in[i].astype(F32)
    z_out[...] = total.astype(BF16)

    for d in range(1, 16):
        i = lax.rem(z + d, 16)
        remote(z_out.at[lax.rem(i, 4)], z_in.at[z], s_gsend.at[2], s_grecv.at[2], at_z(i))
    z_in[z] = z_out[z_lo]
    arrived(z_in.at[pl.ds(0, 15)], s_grecv.at[2])
    total = z_in[0].astype(F32)
    for i in range(1, 16):
        total = total + z_in[i].astype(F32)
    z_all[z_lo] = total.astype(BF16)
    for d in range(1, 4):
        remote(z_all.at[z_lo], z_all.at[z_lo], s_gsend.at[4], s_grecv.at[4], at(z_lo_=turn(z_lo, d)))
    arrived(z_all.at[pl.ds(0, 3)], s_grecv.at[4])
    full[core, chip_xy] = z_all[...]
    for d in range(1, 16):
        piece = full.at[core, chip_xy]
        remote(piece, piece, s_gsend.at[5], s_grecv.at[5], at_xy(lax.rem(chip_xy + d, 16)))
    arrived(full.at[core, pl.ds(0, 15)], s_grecv.at[5])
    remote(full.at[core], full.at[core], s_gsend.at[6], s_grecv.at[6], sibling)

    def finish(whose):
        for g in range(4):
            weight_grad[pl.ds(pl.multiple_of(whose * 256, 256), 256), pl.ds(g * 128, 128)] = (
                full[whose, :, g].reshape(256, 128).astype(F32)
            )

    finish(core)
    arrived(full.at[other], s_grecv.at[6])
    finish(other)

    arrived(plan_out, s_plan.at[0])
    arrived(tile[0], s_tile.at[0])
    for j in range(NC):
        arrived(got[j].at[block, core], s_plan.at[2 + j])
        arrived(got[j].at[pl.ds(0, 15)], s_send.at[j])
        for u in (2 * j, 2 * j + 1):
            arrived(part.at[u, pl.ds(0, 6)], s_y.at[u, 0])
            arrived(quar.at[u, pl.ds(0, 6)], s_q.at[u, 0])
        arrived(cross.at[j], s_cross.at[j, 0])
    arrived(core_out, s_gsend.at[0])
    arrived(half.at[pl.ds(0, 15)], s_gsend.at[1])
    arrived(z_in.at[pl.ds(0, 15)], s_gsend.at[2])
    arrived(z_all.at[pl.ds(0, 3)], s_gsend.at[4])
    arrived(full.at[core, pl.ds(0, 15)], s_gsend.at[5])
    arrived(full.at[core], s_gsend.at[6])


def solution(mesh):
    vmem, smem, hbm = pltpu.VMEM, pltpu.SMEM, pltpu.HBM
    dma = pltpu.SemaphoreType.DMA

    def local(*operands):
        scale = 1.0 / math.sqrt(RBG * BLK * mesh.shape["row"])
        return pl.pallas_call(
            functools.partial(kernel, scale),
            out_shape=(
                jax.ShapeDtypeStruct((OWN, F), BF16),
                jax.ShapeDtypeStruct((F, F), F32),
            ),
            in_specs=[pl.BlockSpec(memory_space=s) for s in (hbm, hbm, smem, smem, hbm, hbm)],
            out_specs=[pl.BlockSpec(memory_space=vmem)] * 2,
            scratch_shapes=[
                vmem((OWN, F), BF16),
                vmem((NC, OWN, FC), BF16),
                [vmem((CBG, 2, OWN, FC), BF16)] * NC,
                [vmem((KMAX, BLK, BLK), BF16)] * 2,
                vmem((F, F), BF16),
                vmem((OWN, F), BF16),
                vmem((8, 128), jnp.int32),
                vmem((8, 128), jnp.int32),
                smem((8, 128), jnp.int32),
                vmem((KMAX + 1, BLK, FC), BF16),
                vmem((2 * NC, RBG, BLK, FC), BF16),
                vmem((2 * NC, 3, BLK, FC), BF16),
                vmem((2 * NC, 3, BLK, FC), BF16),
                vmem((2 * NC, 8, 64, FC), BF16),
                vmem((2 * NC, 3, 64, FC), BF16),
                vmem((2 * NC, 3, 64, FC), BF16),
                vmem((2 * NC, OWN, FC), BF16),
                vmem((NC, OWN, FC), BF16),
                vmem((16, 4, 16, 128), F32),
                vmem((16, 4, 16, 128), BF16),
                vmem((16, 4, 16, 128), BF16),
                vmem((16, 4, 16, 128), BF16),
                vmem((16, 4, 16, 128), BF16),
                vmem((4, 16, 128), BF16),
                vmem((16, 16, 128), BF16),
                vmem((4, 16, 128), BF16),
                vmem((2, 16, 4, 16, 128), BF16),
                dma((NC + 4,)), dma((2 + NC,)), dma((NC,)), dma((2,)),
                dma((NC, 4)), dma((NC, 4)), dma((NC, 4)), dma((NC, 4)), dma((NC, 4)),
                dma((NC,)),
                dma((2 * NC, 5)), dma((2 * NC, 5)), dma((NC, 2)),
                dma((7,)), dma((7,)),
                pltpu.SemaphoreType.REGULAR((2,)),
            ],
            compiler_params=pltpu.CompilerParams(
                collective_id=0, has_side_effects=True, vmem_limit_bytes=48 << 20
            ),
        )(*[
            a if i in (2, 3) else pltpu.with_memory_space_constraint(a, pltpu.HBM)
            for i, a in enumerate(operands)
        ])

    placed = (
        P(("col", "row"), None),
        P("row", "col", None, None, None),
        P("row", "col", None),
        P("row", "col"),
        P(),
        P(("row", "col"), None),
    )
    return jax.shard_map(
        local, mesh=mesh, in_specs=placed, out_specs=(P(("row", "col"), None), P()), check_vma=False
    )
```

```python
import functools
import math

import jax
import jax.numpy as jnp
from jax import lax
from jax.experimental import pallas as pl
from jax.experimental.pallas import tpu as pltpu
from jax.sharding import PartitionSpec as P

F = 512
HALF = F // 2
BLK = 256
RBG = 8
KMAX = 6
CBG = 16
OWN = 128
NC = 2
FC = HALF // NC
MESH = pl.DeviceIdType.MESH
BF16 = jnp.bfloat16
F32 = jnp.float32


def remote(src, dst, send, recv, device):
    copy = pltpu.make_async_remote_copy(
        src_ref=src, dst_ref=dst, send_sem=send, recv_sem=recv, device_id=device, device_id_type=MESH
    )
    copy.start()


def arrived(view, sem):
    pltpu.make_async_copy(view, view, sem).wait()


def plan_of(index, count):
    slot_row, slot_col = [], []
    for k in range(KMAX):
        number = index[0, 0, k]
        slot_row.append(jnp.where(k < count[0, 0], lax.div(number, CBG), RBG))
        slot_col.append(lax.rem(number, CBG))
    rank = []
    for k in range(KMAX):
        before = jnp.int32(0)
        for m in range(KMAX):
            if m != k:
                ahead = slot_row[m] <= slot_row[k] if m < k else slot_row[m] < slot_row[k]
                before = before + jnp.where(ahead, 1, 0)
        rank.append(before)
    take, take_row, take_col = [], [], []
    for s in range(KMAX):
        picked = [jnp.where(rank[k] == s, 1, 0) for k in range(KMAX)]
        take.append(sum(k * picked[k] for k in range(KMAX)))
        take_row.append(sum(slot_row[k] * picked[k] for k in range(KMAX)))
        take_col.append(sum(slot_col[k] * picked[k] for k in range(KMAX)))
    goes_on = [jnp.int32(0)] + [
        jnp.where(take_row[s] == take_row[s - 1], 1, 0) for s in range(1, KMAX)
    ]
    last = []
    for r in range(RBG):
        upto = sum(jnp.where(slot_row[k] <= r, 1, 0) for k in range(KMAX))
        here = sum(jnp.where(slot_row[k] == r, 1, 0) for k in range(KMAX))
        last.append(jnp.where(here > 0, upto - 1, KMAX))
    return take + take_col + goes_on + last


def kernel(
    scale,
    features, tiles, index_in, count, weight, cotangent,
    output, weight_grad,
    staged, swap, got, tile, wts, cot, plan_out, plan_in, plan_s, sums, part, part_l, part_r, quar, quar_l, quar_r, res, cross,
    mine, core_out, core_in, half, xy_in, z_out, z_in, z_all, full,
    s_local, s_plan, s_swap, s_tile, s_z, s_l, s_r, s_top, s_bot, s_send, s_y, s_q, s_cross, s_gsend, s_grecv, s_far, index,
):
    row, col = lax.axis_index("row"), lax.axis_index("col")
    core = lax.rem(row, 2)
    block = lax.div(row, 2)
    x, z_lo = lax.rem(block, 4), lax.div(block, 4)
    y, z_hi = lax.div(col, 4), lax.rem(col, 4)
    other = 1 - core
    chip_xy = x * 4 + y
    z = z_hi * 4 + z_lo

    def at(x_=x, y_=y, z_lo_=z_lo, z_hi_=z_hi, core_=core):
        return ((z_lo_ * 4 + x_) * 2 + core_, y_ * 4 + z_hi_)

    def at_xy(i):
        return at(x_=lax.div(i, 4), y_=lax.rem(i, 4))

    def at_z(i):
        i = lax.rem(i, 16)
        return at(z_lo_=lax.rem(i, 4), z_hi_=lax.div(i, 4))

    def turn(i, d):
        return lax.rem(i + d, 4)

    sibling = at(core_=other)
    x_right, x_left = at(x_=turn(x, 1)), at(x_=turn(x, 3))
    y_right, y_left = at(y_=turn(y, 1)), at(y_=turn(y, 3))

    barrier = pltpu.get_barrier_semaphore()
    near = [sibling, x_right, x_left, y_right, y_left] + [at_z(z + 16 + d) for d in (1, -1, 2, -2, 3, -3)]
    near += [at(x_=turn(x, d), core_=other) for d in (1, 3)] + [at(z_lo_=turn(z_lo, d), core_=other) for d in (1, 2, 3)]
    for device in near:
        pl.semaphore_signal(barrier, inc=1, device_id=device, device_id_type=MESH)

    own = [pltpu.make_async_copy(features, staged, s_local.at[0])]
    later = [
        pltpu.make_async_copy(tiles.at[0, 0], tile[0], s_local.at[NC]),
        pltpu.make_async_copy(weight, wts, s_local.at[NC + 1]),
        pltpu.make_async_copy(cotangent, cot, s_local.at[NC + 2]),
    ]
    scalars = [
        pltpu.make_async_copy(index_in, index, s_local.at[NC + 4]),
    ]
    own[0].start()
    for copy in scalars:
        copy.start()

    sums[KMAX] = jnp.zeros((BLK, FC), BF16)

    def columns(whose, j):
        return staged[:, pl.ds(pl.multiple_of(whose * HALF + j * FC, FC), FC)]

    own[0].wait()
    for j in range(NC):
        swap[j] = columns(other, j)
        got[j][block, core] = columns(core, j)
    pl.semaphore_wait(barrier, 16)
    pl.semaphore_signal(s_far.at[0], inc=1, device_id=at_z(z + 13), device_id_type=MESH)
    pl.semaphore_signal(s_far.at[1], inc=1, device_id=at_z(z + 3), device_id_type=MESH)

    def give(j, p, sem, device):
        remote(got[j].at[p], got[j].at[p], s_send.at[j], sem, device)

    def give_half(j, p, t, sem, device):
        remote(got[j].at[p, t], got[j].at[p, t], s_send.at[j], sem, device)

    def give_own(j, sem, same, crossed):
        remote(got[j].at[block, core], got[j].at[block, core], s_send.at[j], sem, same)
        remote(swap.at[j], got[j].at[block, core], s_send.at[j], sem, crossed)

    def spread_own(j):
        give_own(j, s_l.at[j, 0], x_right, at(x_=turn(x, 1), core_=other))
        give_own(j, s_r.at[j, 0], x_left, at(x_=turn(x, 3), core_=other))

    def spread(j, d):
        p = turn(z_lo, d) * 4 + x
        give(j, p, s_l.at[j, d], x_right)
        give(j, p, s_r.at[j, d], x_left)

    def gather_start(j):
        for d in (1, 3, 2):
            give_own(j, s_z.at[j, 4 - d], at(z_lo_=turn(z_lo, d)), at(z_lo_=turn(z_lo, d), core_=other))

    def gather_z(j):
        for d in range(1, 4):
            arrived(got[j].at[turn(z_lo, d) * 4 + x], s_z.at[j, d])
            spread(j, d)

    def gather_x(j, part=range(4)):
        for d in part:
            line = turn(z_lo, d) * 4
            p_l, p_r = line + turn(x, 3), line + turn(x, 1)
            arrived(got[j].at[p_l], s_l.at[j, d])
            give_half(j, p_l, 0, s_top.at[j, d], x_right)
            arrived(got[j].at[p_r], s_r.at[j, d])
            give_half(j, p_r, 1, s_bot.at[j, d], x_left)

    def gather_end(j):
        arrived(got[j].at[block, other], s_swap.at[j])
        for d in range(4):
            p = turn(z_lo, d) * 4 + turn(x, 2)
            arrived(got[j].at[p, 0], s_top.at[j, d])
            arrived(got[j].at[p, 1], s_bot.at[j, d])

    gather_start(0)
    spread_own(0)
    for j in range(NC):
        remote(swap.at[j], got[j].at[block, core], s_plan.at[2 + j], s_swap.at[j], sibling)
    for copy in later:
        copy.start()
    for copy in scalars:
        copy.wait()
    plan = plan_of(index, count)
    lane = lax.broadcasted_iota(jnp.int32, (8, 128), 1)
    table = jnp.zeros((8, 128), jnp.int32)
    for i, entry in enumerate(plan):
        table = jnp.where(lane == i, entry, table)
    plan_out[...] = table
    remote(plan_out, plan_in, s_plan.at[0], s_plan.at[1], sibling)

    def multiply(u):
        j = u // 2
        entry = (lambda i: plan_s[0, i]) if u % 2 else (lambda i: plan[i])
        for s in range(KMAX):
            features_block = got[j][entry(KMAX + s)].reshape(BLK, FC)
            product = jnp.dot(tile[u % 2][entry(s)], features_block, preferred_element_type=F32)
            if s:
                product = product + jnp.where(entry(2 * KMAX + s) == 1, running, 0.0)
            running = product
            sums[s] = running.astype(BF16)
        for r in range(RBG):
            part[u, r] = sums[entry(3 * KMAX + r)]

    def ring_start(j, buf, from_l, from_r, me, right, left, sems):
        opp = turn(me, 2)
        remote(buf.at[j, 2 * opp], from_l.at[j, 0], sems.at[j, 0], sems.at[j, 1], right)
        remote(buf.at[j, 2 * opp + 1], from_r.at[j, 0], sems.at[j, 0], sems.at[j, 2], left)

    def ring_turn(j, buf, from_l, from_r, me, right, left, sems):
        nxt, prv = turn(me, 1), turn(me, 3)
        arrived(from_l.at[j, 0], sems.at[j, 1])
        buf[j, 2 * nxt] = (buf[j, 2 * nxt].astype(F32) + from_l[j, 0].astype(F32)).astype(BF16)
        remote(buf.at[j, pl.ds(2 * nxt, 2)], from_l.at[j, pl.ds(1, 2)], sems.at[j, 0], sems.at[j, 3], right)
        arrived(from_r.at[j, 0], sems.at[j, 2])
        buf[j, 2 * prv + 1] = (buf[j, 2 * prv + 1].astype(F32) + from_r[j, 0].astype(F32)).astype(BF16)
        remote(buf.at[j, pl.ds(2 * prv, 2)], from_r.at[j, pl.ds(1, 2)], sems.at[j, 0], sems.at[j, 4], left)

    def ring_end(j, buf, from_l, from_r, me, sems):
        arrived(from_l.at[j, pl.ds(1, 2)], sems.at[j, 3])
        arrived(from_r.at[j, pl.ds(1, 2)], sems.at[j, 4])
        return [
            (buf[j, 2 * me + t].astype(F32) + from_l[j, 1 + t].astype(F32) + from_r[j, 1 + t].astype(F32)).astype(BF16)
            for t in range(2)
        ]

    ring_y = (part, part_l, part_r)
    ring_q = (quar, quar_l, quar_r)
    dev_y = (y, y_right, y_left)
    dev_q = (z_hi, at(z_hi_=turn(z_hi, 1)), at(z_hi_=turn(z_hi, 3)))

    def y_start(j):
        ring_start(j, *ring_y, *dev_y, s_y)

    def y_turn(j):
        ring_turn(j, *ring_y, *dev_y, s_y)

    def y_end(j):
        for t, value in enumerate(ring_end(j, *ring_y, y, s_y)):
            for q in range(4):
                quar[j, 4 * t + q] = value[q * 64:(q + 1) * 64]
        ring_start(j, *ring_q, *dev_q, s_q)

    def q_turn(j):
        ring_turn(j, *ring_q, *dev_q, s_q)

    def q_end(u):
        for t, value in enumerate(ring_end(u, *ring_q, z_hi, s_q)):
            res[u, pl.ds(64 * t, 64)] = value
        if u % 2:
            remote(res.at[u], cross.at[u // 2], s_cross.at[u // 2, 0], s_cross.at[u // 2, 1], sibling)

    later[0].wait()
    remote(tile[0], tile[1], s_tile.at[0], s_tile.at[1], sibling)
    arrived(plan_in, s_plan.at[1])
    to_scalars = pltpu.make_async_copy(plan_in, plan_s, s_local.at[NC + 3])
    to_scalars.start()
    gather_z(0)
    gather_start(1)
    gather_x(0)
    spread_own(1)
    gather_end(0)
    gather_z(1)
    multiply(0)
    y_start(0)
    to_scalars.wait()
    arrived(tile[1], s_tile.at[1])
    multiply(1)
    y_start(1)
    gather_x(1, (0, 1))
    y_turn(0)
    y_turn(1)
    pl.semaphore_wait(s_far.at[0], 1)
    pl.semaphore_wait(s_far.at[1], 1)
    y_end(0)
    gather_x(1, (2, 3))
    y_end(1)
    gather_end(1)
    multiply(3)
    y_start(3)
    multiply(2)
    y_start(2)
    q_turn(0)
    y_turn(3)
    q_turn(1)
    y_turn(2)
    y_end(3)
    q_end(0)
    q_end(1)
    y_end(2)
    q_turn(3)
    q_turn(2)
    q_end(3)
    q_end(2)

    later[1].wait()
    later[2].wait()

    def rows_of(whose, j):
        return pl.ds(pl.multiple_of(whose * HALF + j * FC, FC), FC)

    kept = [res[2 * j] for j in range(NC)]
    preact = sum(jnp.dot(kept[j], wts[rows_of(core, j)], preferred_element_type=F32) for j in range(NC))
    for j in range(NC):
        arrived(cross.at[j], s_cross.at[j, 1])
    swapped = [cross[j] for j in range(NC)]
    preact = preact + sum(
        jnp.dot(swapped[j], wts[rows_of(other, j)], preferred_element_type=F32) for j in range(NC)
    )
    low = jnp.minimum(preact, 0.0)
    slope = jnp.exp(low)
    near = low * (1.0 + low * (0.5 + low * (1.0 / 6 + low * (1.0 / 24))))
    output[...] = jnp.where(preact > 0, preact, jnp.where(low > -0.03125, near, slope - 1.0)).astype(BF16)
    grad_pre = (cot[...].astype(F32) * slope).astype(BF16)

    def term(aggregated):
        return scale * lax.dot_general(
            aggregated, grad_pre, (((0,), (0,)), ((), ())), preferred_element_type=F32
        )

    span = FC // 16
    for j in range(NC):
        value = term(swapped[j]).astype(BF16)
        for g in range(4):
            core_out[pl.ds(j * span, span), g] = value[:, g * 128:(g + 1) * 128].reshape(span, 16, 128)
    remote(core_out, core_in, s_gsend.at[0], s_grecv.at[0], sibling)
    for j in range(NC):
        value = term(kept[j])
        for g in range(4):
            mine[pl.ds(j * span, span), g] = value[:, g * 128:(g + 1) * 128].reshape(span, 16, 128)
    arrived(core_in, s_grecv.at[0])
    half[...] = (mine[...] + core_in[...].astype(F32)).astype(BF16)

    hops = (0, 1, 2, 1)
    far_first = sorted(((dx, dy) for dx in range(4) for dy in range(4)), key=lambda d: -hops[d[0]] - hops[d[1]])[:15]
    for dx, dy in far_first:
        i = turn(x, dx) * 4 + turn(y, dy)
        remote(half.at[i], xy_in.at[chip_xy], s_gsend.at[1], s_grecv.at[1], at_xy(i))
    xy_in[chip_xy] = half[chip_xy]
    arrived(xy_in.at[pl.ds(0, 15)], s_grecv.at[1])
    total = xy_in[0].astype(F32)
    for i in range(1, 16):
        total = total + xy_in[i].astype(F32)
    z_out[...] = total.astype(BF16)

    for d in (8, 7, 9, 6, 10, 5, 11, 4, 12, 3, 13, 2, 14, 1, 15):
        i = lax.rem(z + d, 16)
        remote(z_out.at[lax.rem(i, 4)], z_in.at[z], s_gsend.at[2], s_grecv.at[2], at_z(i))
    z_in[z] = z_out[z_lo]
    arrived(z_in.at[pl.ds(0, 15)], s_grecv.at[2])
    total = z_in[0].astype(F32)
    for i in range(1, 16):
        total = total + z_in[i].astype(F32)
    z_all[z_lo] = total.astype(BF16)
    for d in range(1, 4):
        remote(z_all.at[z_lo], z_all.at[z_lo], s_gsend.at[4], s_grecv.at[4], at(z_lo_=turn(z_lo, d)))
    arrived(z_all.at[pl.ds(0, 3)], s_grecv.at[4])
    full[core, chip_xy] = z_all[...]
    piece = full.at[core, chip_xy]
    for dx, dy in far_first:
        remote(piece, piece, s_gsend.at[5], s_grecv.at[5], at(x_=turn(x, dx), y_=turn(y, dy)))
    arrived(full.at[core, pl.ds(0, 15)], s_grecv.at[5])
    remote(full.at[core], full.at[core], s_gsend.at[6], s_grecv.at[6], sibling)

    def finish(whose):
        for g in range(4):
            weight_grad[pl.ds(pl.multiple_of(whose * 256, 256), 256), pl.ds(g * 128, 128)] = (
                full[whose, :, g].reshape(256, 128).astype(F32)
            )

    finish(core)
    arrived(full.at[other], s_grecv.at[6])
    finish(other)

    arrived(plan_out, s_plan.at[0])
    arrived(tile[0], s_tile.at[0])
    for j in range(NC):
        arrived(got[j].at[block, core], s_plan.at[2 + j])
        arrived(got[j].at[pl.ds(0, 15)], s_send.at[j])
        for u in (2 * j, 2 * j + 1):
            arrived(part.at[u, pl.ds(0, 6)], s_y.at[u, 0])
            arrived(quar.at[u, pl.ds(0, 6)], s_q.at[u, 0])
        arrived(cross.at[j], s_cross.at[j, 0])
    arrived(core_out, s_gsend.at[0])
    arrived(half.at[pl.ds(0, 15)], s_gsend.at[1])
    arrived(z_in.at[pl.ds(0, 15)], s_gsend.at[2])
    arrived(z_all.at[pl.ds(0, 3)], s_gsend.at[4])
    arrived(full.at[core, pl.ds(0, 15)], s_gsend.at[5])
    arrived(full.at[core], s_gsend.at[6])


def solution(mesh):
    vmem, smem, hbm = pltpu.VMEM, pltpu.SMEM, pltpu.HBM
    dma = pltpu.SemaphoreType.DMA

    def local(*operands):
        scale = 1.0 / math.sqrt(RBG * BLK * mesh.shape["row"])
        return pl.pallas_call(
            functools.partial(kernel, scale),
            out_shape=(
                jax.ShapeDtypeStruct((OWN, F), BF16),
                jax.ShapeDtypeStruct((F, F), F32),
            ),
            in_specs=[pl.BlockSpec(memory_space=s) for s in (hbm, hbm, hbm, smem, hbm, hbm)],
            out_specs=[pl.BlockSpec(memory_space=vmem)] * 2,
            scratch_shapes=[
                vmem((OWN, F), BF16),
                vmem((NC, OWN, FC), BF16),
                [vmem((CBG, 2, OWN, FC), BF16)] * NC,
                [vmem((KMAX, BLK, BLK), BF16)] * 2,
                vmem((F, F), BF16),
                vmem((OWN, F), BF16),
                vmem((8, 128), jnp.int32),
                vmem((8, 128), jnp.int32),
                smem((8, 128), jnp.int32),
                vmem((KMAX + 1, BLK, FC), BF16),
                vmem((2 * NC, RBG, BLK, FC), BF16),
                vmem((2 * NC, 3, BLK, FC), BF16),
                vmem((2 * NC, 3, BLK, FC), BF16),
                vmem((2 * NC, 8, 64, FC), BF16),
                vmem((2 * NC, 3, 64, FC), BF16),
                vmem((2 * NC, 3, 64, FC), BF16),
                vmem((2 * NC, OWN, FC), BF16),
                vmem((NC, OWN, FC), BF16),
                vmem((16, 4, 16, 128), F32),
                vmem((16, 4, 16, 128), BF16),
                vmem((16, 4, 16, 128), BF16),
                vmem((16, 4, 16, 128), BF16),
                vmem((16, 4, 16, 128), BF16),
                vmem((4, 16, 128), BF16),
                vmem((16, 16, 128), BF16),
                vmem((4, 16, 128), BF16),
                vmem((2, 16, 4, 16, 128), BF16),
                dma((NC + 5,)), dma((2 + NC,)), dma((NC,)), dma((2,)),
                dma((NC, 4)), dma((NC, 4)), dma((NC, 4)), dma((NC, 4)), dma((NC, 4)),
                dma((NC,)),
                dma((2 * NC, 5)), dma((2 * NC, 5)), dma((NC, 2)),
                dma((7,)), dma((7,)),
                pltpu.SemaphoreType.REGULAR((2,)),
                smem((1, 1, KMAX), jnp.int32),
            ],
            compiler_params=pltpu.CompilerParams(
                collective_id=0, has_side_effects=True, vmem_limit_bytes=48 << 20
            ),
        )(*[
            a if i == 3 else pltpu.with_memory_space_constraint(a, pltpu.HBM)
            for i, a in enumerate(operands)
        ])

    placed = (
        P(("col", "row"), None),
        P("row", "col", None, None, None),
        P("row", "col", None),
        P("row", "col"),
        P(),
        P(("row", "col"), None),
    )
    return jax.shard_map(
        local, mesh=mesh, in_specs=placed, out_specs=(P(("row", "col"), None), P()), check_vma=False
    )
```

```python
import functools
import math

import jax
import jax.numpy as jnp
from jax import lax
from jax.experimental import pallas as pl
from jax.experimental.pallas import tpu as pltpu
from jax.sharding import PartitionSpec as P

F = 512
HALF = F // 2
BLK = 256
RBG = 8
KMAX = 6
CBG = 16
OWN = 128
NC = 2
FC = HALF // NC
MESH = pl.DeviceIdType.MESH
BF16 = jnp.bfloat16
F32 = jnp.float32


def remote(src, dst, send, recv, device):
    copy = pltpu.make_async_remote_copy(
        src_ref=src, dst_ref=dst, send_sem=send, recv_sem=recv, device_id=device, device_id_type=MESH
    )
    copy.start()


def arrived(view, sem):
    pltpu.make_async_copy(view, view, sem).wait()


def plan_of(index, count):
    slot_row, slot_col = [], []
    for k in range(KMAX):
        number = index[0, 0, k]
        slot_row.append(jnp.where(k < count[0, 0], lax.div(number, CBG), RBG))
        slot_col.append(lax.rem(number, CBG))
    rank = []
    for k in range(KMAX):
        before = jnp.int32(0)
        for m in range(KMAX):
            if m != k:
                ahead = slot_row[m] <= slot_row[k] if m < k else slot_row[m] < slot_row[k]
                before = before + jnp.where(ahead, 1, 0)
        rank.append(before)
    take, take_row, take_col = [], [], []
    for s in range(KMAX):
        picked = [jnp.where(rank[k] == s, 1, 0) for k in range(KMAX)]
        take.append(sum(k * picked[k] for k in range(KMAX)))
        take_row.append(sum(slot_row[k] * picked[k] for k in range(KMAX)))
        take_col.append(sum(slot_col[k] * picked[k] for k in range(KMAX)))
    goes_on = [jnp.int32(0)] + [
        jnp.where(take_row[s] == take_row[s - 1], 1, 0) for s in range(1, KMAX)
    ]
    last = []
    for r in range(RBG):
        upto = sum(jnp.where(slot_row[k] <= r, 1, 0) for k in range(KMAX))
        here = sum(jnp.where(slot_row[k] == r, 1, 0) for k in range(KMAX))
        last.append(jnp.where(here > 0, upto - 1, KMAX))
    return take + take_col + goes_on + last


def kernel(
    scale,
    features, tiles, index_in, count, weight, cotangent,
    output, weight_grad,
    staged, swap, got, tile, wts, cot, plan_out, plan_in, plan_s, sums, part, part_l, part_r, quar, quar_l, quar_r, res, cross,
    mine, core_out, core_in, half, xy_in, z_out, z_in, z_all, full,
    s_local, s_plan, s_swap, s_tile, s_z, s_l, s_r, s_top, s_bot, s_send, s_y, s_q, s_cross, s_gsend, s_grecv, s_far, index,
):
    row, col = lax.axis_index("row"), lax.axis_index("col")
    core = lax.rem(row, 2)
    block = lax.div(row, 2)
    x, z_lo = lax.rem(block, 4), lax.div(block, 4)
    y, z_hi = lax.div(col, 4), lax.rem(col, 4)
    other = 1 - core
    chip_xy = x * 4 + y
    z = z_hi * 4 + z_lo

    def at(x_=x, y_=y, z_lo_=z_lo, z_hi_=z_hi, core_=core):
        return ((z_lo_ * 4 + x_) * 2 + core_, y_ * 4 + z_hi_)

    def at_xy(i):
        return at(x_=lax.div(i, 4), y_=lax.rem(i, 4))

    def at_z(i):
        i = lax.rem(i, 16)
        return at(z_lo_=lax.rem(i, 4), z_hi_=lax.div(i, 4))

    def turn(i, d):
        return lax.rem(i + d, 4)

    sibling = at(core_=other)
    x_right, x_left = at(x_=turn(x, 1)), at(x_=turn(x, 3))
    y_right, y_left = at(y_=turn(y, 1)), at(y_=turn(y, 3))

    barrier = pltpu.get_barrier_semaphore()
    near = [sibling, x_right, x_left, y_right, y_left] + [at_z(z + 16 + d) for d in (3, -3, 2, -2, 1, -1)]
    near += [at(x_=turn(x, d), core_=other) for d in (1, 3)] + [at(z_lo_=turn(z_lo, d), core_=other) for d in (1, 2, 3)]
    for device in near[::-1]:
        pl.semaphore_signal(barrier, inc=1, device_id=device, device_id_type=MESH)

    own = [pltpu.make_async_copy(features, staged, s_local.at[0])]
    later = [
        pltpu.make_async_copy(tiles.at[0, 0], tile[0], s_local.at[NC]),
        pltpu.make_async_copy(weight, wts, s_local.at[NC + 1]),
        pltpu.make_async_copy(cotangent, cot, s_local.at[NC + 2]),
    ]
    scalars = [
        pltpu.make_async_copy(index_in, index, s_local.at[NC + 4]),
    ]
    own[0].start()
    for copy in scalars:
        copy.start()

    sums[KMAX] = jnp.zeros((BLK, FC), BF16)

    def columns(whose, j):
        return staged[:, pl.ds(pl.multiple_of(whose * HALF + j * FC, FC), FC)]

    own[0].wait()
    for j in range(NC):
        swap[j] = columns(other, j)
        got[j][block, core] = columns(core, j)
    pl.semaphore_wait(barrier, 16)
    pl.semaphore_signal(s_far.at[0], inc=1, device_id=at_z(z + 13), device_id_type=MESH)
    pl.semaphore_signal(s_far.at[1], inc=1, device_id=at_z(z + 3), device_id_type=MESH)

    def give(j, p, sem, device):
        remote(got[j].at[p], got[j].at[p], s_send.at[j], sem, device)

    def give_half(j, p, t, sem, device):
        remote(got[j].at[p, t], got[j].at[p, t], s_send.at[j], sem, device)

    def give_own(j, sem, same, crossed):
        remote(got[j].at[block, core], got[j].at[block, core], s_send.at[j], sem, same)
        remote(swap.at[j], got[j].at[block, core], s_send.at[j], sem, crossed)

    def spread_own(j):
        give_own(j, s_l.at[j, 0], x_right, at(x_=turn(x, 1), core_=other))
        give_own(j, s_r.at[j, 0], x_left, at(x_=turn(x, 3), core_=other))

    def spread(j, d):
        p = turn(z_lo, d) * 4 + x
        give(j, p, s_l.at[j, d], x_right)
        give(j, p, s_r.at[j, d], x_left)

    def gather_start(j):
        for d in (2, 3, 1):
            give_own(j, s_z.at[j, 4 - d], at(z_lo_=turn(z_lo, d)), at(z_lo_=turn(z_lo, d), core_=other))

    def gather_z(j, part=(1, 2, 3)):
        for d in part:
            arrived(got[j].at[turn(z_lo, d) * 4 + x], s_z.at[j, d])
            spread(j, d)

    def gather_x(j, part=range(4)):
        for d in part:
            line = turn(z_lo, d) * 4
            p_l, p_r = line + turn(x, 3), line + turn(x, 1)
            arrived(got[j].at[p_l], s_l.at[j, d])
            give_half(j, p_l, 0, s_top.at[j, d], x_right)
            arrived(got[j].at[p_r], s_r.at[j, d])
            give_half(j, p_r, 1, s_bot.at[j, d], x_left)

    def gather_end(j):
        arrived(got[j].at[block, other], s_swap.at[j])
        for d in range(4):
            p = turn(z_lo, d) * 4 + turn(x, 2)
            arrived(got[j].at[p, 0], s_top.at[j, d])
            arrived(got[j].at[p, 1], s_bot.at[j, d])

    gather_start(0)
    spread_own(0)
    for j in range(NC):
        remote(swap.at[j], got[j].at[block, core], s_plan.at[2 + j], s_swap.at[j], sibling)
    for copy in later:
        copy.start()
    for copy in scalars:
        copy.wait()
    plan = plan_of(index, count)
    lane = lax.broadcasted_iota(jnp.int32, (8, 128), 1)
    table = jnp.zeros((8, 128), jnp.int32)
    for i, entry in enumerate(plan):
        table = jnp.where(lane == i, entry, table)
    plan_out[...] = table
    remote(plan_out, plan_in, s_plan.at[0], s_plan.at[1], sibling)

    def multiply(u):
        j = u // 2
        entry = (lambda i: plan_s[0, i]) if u % 2 else (lambda i: plan[i])
        for s in range(KMAX):
            features_block = got[j][entry(KMAX + s)].reshape(BLK, FC)
            product = jnp.dot(tile[u % 2][entry(s)], features_block, preferred_element_type=F32)
            if s:
                product = product + jnp.where(entry(2 * KMAX + s) == 1, running, 0.0)
            running = product
            sums[s] = running.astype(BF16)
        for r in range(RBG):
            part[u, r] = sums[entry(3 * KMAX + r)]

    def ring_start(j, buf, from_l, from_r, me, right, left, sems):
        opp = turn(me, 2)
        remote(buf.at[j, 2 * opp], from_l.at[j, 0], sems.at[j, 0], sems.at[j, 1], right)
        remote(buf.at[j, 2 * opp + 1], from_r.at[j, 0], sems.at[j, 0], sems.at[j, 2], left)

    def ring_turn(j, buf, from_l, from_r, me, right, left, sems):
        nxt, prv = turn(me, 1), turn(me, 3)
        arrived(from_l.at[j, 0], sems.at[j, 1])
        buf[j, 2 * nxt] = (buf[j, 2 * nxt].astype(F32) + from_l[j, 0].astype(F32)).astype(BF16)
        remote(buf.at[j, pl.ds(2 * nxt, 2)], from_l.at[j, pl.ds(1, 2)], sems.at[j, 0], sems.at[j, 3], right)
        arrived(from_r.at[j, 0], sems.at[j, 2])
        buf[j, 2 * prv + 1] = (buf[j, 2 * prv + 1].astype(F32) + from_r[j, 0].astype(F32)).astype(BF16)
        remote(buf.at[j, pl.ds(2 * prv, 2)], from_r.at[j, pl.ds(1, 2)], sems.at[j, 0], sems.at[j, 4], left)

    def ring_end(j, buf, from_l, from_r, me, sems):
        arrived(from_l.at[j, pl.ds(1, 2)], sems.at[j, 3])
        arrived(from_r.at[j, pl.ds(1, 2)], sems.at[j, 4])
        return [
            (buf[j, 2 * me + t].astype(F32) + from_l[j, 1 + t].astype(F32) + from_r[j, 1 + t].astype(F32)).astype(BF16)
            for t in range(2)
        ]

    ring_y = (part, part_l, part_r)
    ring_q = (quar, quar_l, quar_r)
    dev_y = (y, y_right, y_left)
    dev_q = (z_hi, at(z_hi_=turn(z_hi, 1)), at(z_hi_=turn(z_hi, 3)))

    def y_start(j):
        ring_start(j, *ring_y, *dev_y, s_y)

    def y_turn(j):
        ring_turn(j, *ring_y, *dev_y, s_y)

    def y_end(j):
        for t, value in enumerate(ring_end(j, *ring_y, y, s_y)):
            for q in range(4):
                quar[j, 4 * t + q] = value[q * 64:(q + 1) * 64]
        ring_start(j, *ring_q, *dev_q, s_q)

    def q_turn(j):
        ring_turn(j, *ring_q, *dev_q, s_q)

    def q_end(u):
        for t, value in enumerate(ring_end(u, *ring_q, z_hi, s_q)):
            res[u, pl.ds(64 * t, 64)] = value
        if u % 2:
            remote(res.at[u], cross.at[u // 2], s_cross.at[u // 2, 0], s_cross.at[u // 2, 1], sibling)

    later[0].wait()
    remote(tile[0], tile[1], s_tile.at[0], s_tile.at[1], sibling)
    arrived(plan_in, s_plan.at[1])
    to_scalars = pltpu.make_async_copy(plan_in, plan_s, s_local.at[NC + 3])
    to_scalars.start()
    gather_z(0)
    gather_start(1)
    gather_x(0)
    spread_own(1)
    gather_end(0)
    gather_z(1)
    multiply(0)
    y_start(0)
    to_scalars.wait()
    arrived(tile[1], s_tile.at[1])
    multiply(1)
    y_start(1)
    gather_x(1, (0, 1))
    y_turn(0)
    y_turn(1)
    pl.semaphore_wait(s_far.at[0], 1)
    pl.semaphore_wait(s_far.at[1], 1)
    y_end(0)
    gather_x(1, (2, 3))
    y_end(1)
    gather_end(1)
    multiply(3)
    y_start(3)
    multiply(2)
    y_start(2)
    q_turn(0)
    y_turn(3)
    q_turn(1)
    y_turn(2)
    y_end(3)
    q_end(0)
    q_end(1)
    y_end(2)
    q_turn(3)
    q_turn(2)
    q_end(3)
    q_end(2)

    later[1].wait()
    later[2].wait()

    def rows_of(whose, j):
        return pl.ds(pl.multiple_of(whose * HALF + j * FC, FC), FC)

    kept = [res[2 * j] for j in range(NC)]
    preact = sum(jnp.dot(kept[j], wts[rows_of(core, j)], preferred_element_type=F32) for j in range(NC))
    for j in range(NC):
        arrived(cross.at[j], s_cross.at[j, 1])
    swapped = [cross[j] for j in range(NC)]
    preact = preact + sum(
        jnp.dot(swapped[j], wts[rows_of(other, j)], preferred_element_type=F32) for j in range(NC)
    )
    low = jnp.minimum(preact, 0.0)
    slope = jnp.exp(low)
    near = low * (1.0 + low * (0.5 + low * (1.0 / 6 + low * (1.0 / 24))))
    output[...] = jnp.where(preact > 0, preact, jnp.where(low > -0.03125, near, slope - 1.0)).astype(BF16)
    grad_pre = (cot[...].astype(F32) * slope).astype(BF16)

    def term(aggregated):
        return scale * lax.dot_general(
            aggregated, grad_pre, (((0,), (0,)), ((), ())), preferred_element_type=F32
        )

    span = FC // 16
    for j in range(NC):
        value = term(swapped[j]).astype(BF16)
        for g in range(4):
            core_out[pl.ds(j * span, span), g] = value[:, g * 128:(g + 1) * 128].reshape(span, 16, 128)
    remote(core_out, core_in, s_gsend.at[0], s_grecv.at[0], sibling)
    for j in range(NC):
        value = term(kept[j])
        for g in range(4):
            mine[pl.ds(j * span, span), g] = value[:, g * 128:(g + 1) * 128].reshape(span, 16, 128)
    arrived(core_in, s_grecv.at[0])
    half[...] = (mine[...] + core_in[...].astype(F32)).astype(BF16)

    hops = (0, 1, 2, 1)
    far_first = sorted(((dx, dy) for dx in range(4) for dy in range(4)), key=lambda d: -hops[d[0]] - hops[d[1]])[:15]
    for dx, dy in far_first:
        i = turn(x, dx) * 4 + turn(y, dy)
        remote(half.at[i], xy_in.at[chip_xy], s_gsend.at[1], s_grecv.at[1], at_xy(i))
    xy_in[chip_xy] = half[chip_xy]
    arrived(xy_in.at[pl.ds(0, 15)], s_grecv.at[1])
    total = xy_in[0].astype(F32)
    for i in range(1, 16):
        total = total + xy_in[i].astype(F32)
    z_out[...] = total.astype(BF16)

    for d in (8, 7, 9, 6, 10, 5, 11, 4, 12, 3, 13, 2, 14, 1, 15):
        i = lax.rem(z + d, 16)
        remote(z_out.at[lax.rem(i, 4)], z_in.at[z], s_gsend.at[2], s_grecv.at[2], at_z(i))
    z_in[z] = z_out[z_lo]
    arrived(z_in.at[pl.ds(0, 15)], s_grecv.at[2])
    total = z_in[0].astype(F32)
    for i in range(1, 16):
        total = total + z_in[i].astype(F32)
    z_all[z_lo] = total.astype(BF16)
    for d in range(1, 4):
        remote(z_all.at[z_lo], z_all.at[z_lo], s_gsend.at[4], s_grecv.at[4], at(z_lo_=turn(z_lo, d)))
    arrived(z_all.at[pl.ds(0, 3)], s_grecv.at[4])
    full[core, chip_xy] = z_all[...]
    piece = full.at[core, chip_xy]
    for dx, dy in far_first:
        remote(piece, piece, s_gsend.at[5], s_grecv.at[5], at(x_=turn(x, dx), y_=turn(y, dy)))
    arrived(full.at[core, pl.ds(0, 15)], s_grecv.at[5])
    remote(full.at[core], full.at[core], s_gsend.at[6], s_grecv.at[6], sibling)

    def finish(whose):
        for g in range(4):
            weight_grad[pl.ds(pl.multiple_of(whose * 256, 256), 256), pl.ds(g * 128, 128)] = (
                full[whose, :, g].reshape(256, 128).astype(F32)
            )

    finish(core)
    arrived(full.at[other], s_grecv.at[6])
    finish(other)

    arrived(plan_out, s_plan.at[0])
    arrived(tile[0], s_tile.at[0])
    for j in range(NC):
        arrived(got[j].at[block, core], s_plan.at[2 + j])
        arrived(got[j].at[pl.ds(0, 15)], s_send.at[j])
        for u in (2 * j, 2 * j + 1):
            arrived(part.at[u, pl.ds(0, 6)], s_y.at[u, 0])
            arrived(quar.at[u, pl.ds(0, 6)], s_q.at[u, 0])
        arrived(cross.at[j], s_cross.at[j, 0])
    arrived(core_out, s_gsend.at[0])
    arrived(half.at[pl.ds(0, 15)], s_gsend.at[1])
    arrived(z_in.at[pl.ds(0, 15)], s_gsend.at[2])
    arrived(z_all.at[pl.ds(0, 3)], s_gsend.at[4])
    arrived(full.at[core, pl.ds(0, 15)], s_gsend.at[5])
    arrived(full.at[core], s_gsend.at[6])


def solution(mesh):
    vmem, smem, hbm = pltpu.VMEM, pltpu.SMEM, pltpu.HBM
    dma = pltpu.SemaphoreType.DMA

    def local(*operands):
        scale = 1.0 / math.sqrt(RBG * BLK * mesh.shape["row"])
        return pl.pallas_call(
            functools.partial(kernel, scale),
            out_shape=(
                jax.ShapeDtypeStruct((OWN, F), BF16),
                jax.ShapeDtypeStruct((F, F), F32),
            ),
            in_specs=[pl.BlockSpec(memory_space=s) for s in (hbm, hbm, hbm, smem, hbm, hbm)],
            out_specs=[pl.BlockSpec(memory_space=vmem)] * 2,
            scratch_shapes=[
                vmem((OWN, F), BF16),
                vmem((NC, OWN, FC), BF16),
                [vmem((CBG, 2, OWN, FC), BF16)] * NC,
                [vmem((KMAX, BLK, BLK), BF16)] * 2,
                vmem((F, F), BF16),
                vmem((OWN, F), BF16),
                vmem((8, 128), jnp.int32),
                vmem((8, 128), jnp.int32),
                smem((8, 128), jnp.int32),
                vmem((KMAX + 1, BLK, FC), BF16),
                vmem((2 * NC, RBG, BLK, FC), BF16),
                vmem((2 * NC, 3, BLK, FC), BF16),
                vmem((2 * NC, 3, BLK, FC), BF16),
                vmem((2 * NC, 8, 64, FC), BF16),
                vmem((2 * NC, 3, 64, FC), BF16),
                vmem((2 * NC, 3, 64, FC), BF16),
                vmem((2 * NC, OWN, FC), BF16),
                vmem((NC, OWN, FC), BF16),
                vmem((16, 4, 16, 128), F32),
                vmem((16, 4, 16, 128), BF16),
                vmem((16, 4, 16, 128), BF16),
                vmem((16, 4, 16, 128), BF16),
                vmem((16, 4, 16, 128), BF16),
                vmem((4, 16, 128), BF16),
                vmem((16, 16, 128), BF16),
                vmem((4, 16, 128), BF16),
                vmem((2, 16, 4, 16, 128), BF16),
                dma((NC + 5,)), dma((2 + NC,)), dma((NC,)), dma((2,)),
                dma((NC, 4)), dma((NC, 4)), dma((NC, 4)), dma((NC, 4)), dma((NC, 4)),
                dma((NC,)),
                dma((2 * NC, 5)), dma((2 * NC, 5)), dma((NC, 2)),
                dma((7,)), dma((7,)),
                pltpu.SemaphoreType.REGULAR((2,)),
                smem((1, 1, KMAX), jnp.int32),
            ],
            compiler_params=pltpu.CompilerParams(
                collective_id=0, has_side_effects=True, vmem_limit_bytes=48 << 20
            ),
        )(*[
            a if i == 3 else pltpu.with_memory_space_constraint(a, pltpu.HBM)
            for i, a in enumerate(operands)
        ])

    placed = (
        P(("col", "row"), None),
        P("row", "col", None, None, None),
        P("row", "col", None),
        P("row", "col"),
        P(),
        P(("row", "col"), None),
    )
    return jax.shard_map(
        local, mesh=mesh, in_specs=placed, out_specs=(P(("row", "col"), None), P()), check_vma=False
    )
```

```python
import functools
import math

import jax
import jax.numpy as jnp
from jax import lax
from jax.experimental import pallas as pl
from jax.experimental.pallas import tpu as pltpu
from jax.sharding import PartitionSpec as P

F = 512
HALF = F // 2
BLK = 256
RBG = 8
KMAX = 6
CBG = 16
OWN = 128
NC = 2
FC = HALF // NC
MESH = pl.DeviceIdType.MESH
BF16 = jnp.bfloat16
F32 = jnp.float32


def remote(src, dst, send, recv, device):
    copy = pltpu.make_async_remote_copy(
        src_ref=src, dst_ref=dst, send_sem=send, recv_sem=recv, device_id=device, device_id_type=MESH
    )
    copy.start()


def arrived(view, sem):
    pltpu.make_async_copy(view, view, sem).wait()


def plan_of(index, count):
    slot_row, slot_col = [], []
    for k in range(KMAX):
        number = index[0, 0, k]
        slot_row.append(jnp.where(k < count[0, 0], lax.div(number, CBG), RBG))
        slot_col.append(lax.rem(number, CBG))
    rank = []
    for k in range(KMAX):
        before = jnp.int32(0)
        for m in range(KMAX):
            if m != k:
                ahead = slot_row[m] <= slot_row[k] if m < k else slot_row[m] < slot_row[k]
                before = before + jnp.where(ahead, 1, 0)
        rank.append(before)
    take, take_row, take_col = [], [], []
    for s in range(KMAX):
        picked = [jnp.where(rank[k] == s, 1, 0) for k in range(KMAX)]
        take.append(sum(k * picked[k] for k in range(KMAX)))
        take_row.append(sum(slot_row[k] * picked[k] for k in range(KMAX)))
        take_col.append(sum(slot_col[k] * picked[k] for k in range(KMAX)))
    goes_on = [jnp.int32(0)] + [
        jnp.where(take_row[s] == take_row[s - 1], 1, 0) for s in range(1, KMAX)
    ]
    last = []
    for r in range(RBG):
        upto = sum(jnp.where(slot_row[k] <= r, 1, 0) for k in range(KMAX))
        here = sum(jnp.where(slot_row[k] == r, 1, 0) for k in range(KMAX))
        last.append(jnp.where(here > 0, upto - 1, KMAX))
    return take + take_col + goes_on + last


def kernel(
    scale,
    features, tiles, index_in, count, weight, cotangent,
    output, weight_grad,
    staged, swap, got, tile, wts, cot, plan_out, plan_in, plan_s, sums, part, part_l, part_r, quar, quar_l, quar_r, res, cross,
    mine, core_out, core_in, half, xy_in, z_out, z_in, z_all, full,
    s_local, s_plan, s_swap, s_tile, s_z, s_l, s_r, s_top, s_bot, s_send, s_y, s_q, s_cross, s_gsend, s_grecv, s_far, index,
):
    row, col = lax.axis_index("row"), lax.axis_index("col")
    core = lax.rem(row, 2)
    block = lax.div(row, 2)
    x, z_lo = lax.rem(block, 4), lax.div(block, 4)
    y, z_hi = lax.div(col, 4), lax.rem(col, 4)
    other = 1 - core
    chip_xy = x * 4 + y
    z = z_hi * 4 + z_lo

    def at(x_=x, y_=y, z_lo_=z_lo, z_hi_=z_hi, core_=core):
        return ((z_lo_ * 4 + x_) * 2 + core_, y_ * 4 + z_hi_)

    def at_xy(i):
        return at(x_=lax.div(i, 4), y_=lax.rem(i, 4))

    def at_z(i):
        i = lax.rem(i, 16)
        return at(z_lo_=lax.rem(i, 4), z_hi_=lax.div(i, 4))

    def turn(i, d):
        return lax.rem(i + d, 4)

    sibling = at(core_=other)
    x_right, x_left = at(x_=turn(x, 1)), at(x_=turn(x, 3))
    y_right, y_left = at(y_=turn(y, 1)), at(y_=turn(y, 3))

    barrier = pltpu.get_barrier_semaphore()
    near = [sibling, x_right, x_left, y_right, y_left] + [at_z(z + 16 + d) for d in (3, -3, 2, -2, 1, -1)]
    near += [at(x_=turn(x, d), core_=other) for d in (1, 3)] + [at(z_lo_=turn(z_lo, d), core_=other) for d in (1, 2, 3)]
    for device in near[::-1]:
        pl.semaphore_signal(barrier, inc=1, device_id=device, device_id_type=MESH)

    own = [pltpu.make_async_copy(features, staged, s_local.at[0])]
    later = [
        pltpu.make_async_copy(tiles.at[0, 0], tile[0], s_local.at[NC]),
        pltpu.make_async_copy(weight, wts, s_local.at[NC + 1]),
        pltpu.make_async_copy(cotangent, cot, s_local.at[NC + 2]),
    ]
    scalars = [
        pltpu.make_async_copy(index_in, index, s_local.at[NC + 4]),
    ]
    own[0].start()
    for copy in scalars:
        copy.start()

    sums[KMAX] = jnp.zeros((BLK, FC), BF16)

    def columns(whose, j):
        return staged[:, pl.ds(pl.multiple_of(whose * HALF + j * FC, FC), FC)]

    own[0].wait()
    for j in range(NC):
        swap[j] = columns(other, j)
        got[j][block, core] = columns(core, j)
    pl.semaphore_wait(barrier, 16)
    pl.semaphore_signal(s_far.at[0], inc=1, device_id=at_z(z + 13), device_id_type=MESH)
    pl.semaphore_signal(s_far.at[1], inc=1, device_id=at_z(z + 3), device_id_type=MESH)

    def give(j, p, sem, device):
        remote(got[j].at[p], got[j].at[p], s_send.at[j], sem, device)

    def give_half(j, p, t, sem, device):
        remote(got[j].at[p, t], got[j].at[p, t], s_send.at[j], sem, device)

    def give_own(j, sem, same, crossed):
        remote(got[j].at[block, core], got[j].at[block, core], s_send.at[j], sem, same)
        remote(swap.at[j], got[j].at[block, core], s_send.at[j], sem, crossed)

    def spread_own(j):
        give_own(j, s_l.at[j, 0], x_right, at(x_=turn(x, 1), core_=other))
        give_own(j, s_r.at[j, 0], x_left, at(x_=turn(x, 3), core_=other))

    def spread(j, d):
        p = turn(z_lo, d) * 4 + x
        give(j, p, s_l.at[j, d], x_right)
        give(j, p, s_r.at[j, d], x_left)

    def gather_start(j):
        for d in (2, 3, 1):
            give_own(j, s_z.at[j, 4 - d], at(z_lo_=turn(z_lo, d)), at(z_lo_=turn(z_lo, d), core_=other))

    def gather_z(j, part=(1, 2, 3)):
        for d in part:
            arrived(got[j].at[turn(z_lo, d) * 4 + x], s_z.at[j, d])
            spread(j, d)

    def gather_x(j, part=range(4)):
        for d in part:
            line = turn(z_lo, d) * 4
            p_l, p_r = line + turn(x, 3), line + turn(x, 1)
            arrived(got[j].at[p_l], s_l.at[j, d])
            give_half(j, p_l, 0, s_top.at[j, d], x_right)
            arrived(got[j].at[p_r], s_r.at[j, d])
            give_half(j, p_r, 1, s_bot.at[j, d], x_left)

    def gather_end(j):
        arrived(got[j].at[block, other], s_swap.at[j])
        for d in range(4):
            p = turn(z_lo, d) * 4 + turn(x, 2)
            arrived(got[j].at[p, 0], s_top.at[j, d])
            arrived(got[j].at[p, 1], s_bot.at[j, d])

    gather_start(0)
    spread_own(0)
    for j in range(NC):
        remote(swap.at[j], got[j].at[block, core], s_plan.at[2 + j], s_swap.at[j], sibling)
    for copy in later:
        copy.start()
    for copy in scalars:
        copy.wait()
    plan = plan_of(index, count)
    lane = lax.broadcasted_iota(jnp.int32, (8, 128), 1)
    table = jnp.zeros((8, 128), jnp.int32)
    for i, entry in enumerate(plan):
        table = jnp.where(lane == i, entry, table)
    plan_out[...] = table
    remote(plan_out, plan_in, s_plan.at[0], s_plan.at[1], sibling)

    def multiply(u):
        j = u // 2
        entry = (lambda i: plan_s[0, i]) if u % 2 else (lambda i: plan[i])
        for s in range(KMAX):
            features_block = got[j][entry(KMAX + s)].reshape(BLK, FC)
            product = jnp.dot(tile[u % 2][entry(s)], features_block, preferred_element_type=F32)
            if s:
                product = product + jnp.where(entry(2 * KMAX + s) == 1, running, 0.0)
            running = product
            sums[s] = running.astype(BF16)
        for r in range(RBG):
            part[u, r] = sums[entry(3 * KMAX + r)]

    def ring_start(j, buf, from_l, from_r, me, right, left, sems):
        opp = turn(me, 2)
        remote(buf.at[j, 2 * opp], from_l.at[j, 0], sems.at[j, 0], sems.at[j, 1], right)
        remote(buf.at[j, 2 * opp + 1], from_r.at[j, 0], sems.at[j, 0], sems.at[j, 2], left)

    def ring_turn(j, buf, from_l, from_r, me, right, left, sems):
        nxt, prv = turn(me, 1), turn(me, 3)
        arrived(from_l.at[j, 0], sems.at[j, 1])
        buf[j, 2 * nxt] = (buf[j, 2 * nxt].astype(F32) + from_l[j, 0].astype(F32)).astype(BF16)
        remote(buf.at[j, pl.ds(2 * nxt, 2)], from_l.at[j, pl.ds(1, 2)], sems.at[j, 0], sems.at[j, 3], right)
        arrived(from_r.at[j, 0], sems.at[j, 2])
        buf[j, 2 * prv + 1] = (buf[j, 2 * prv + 1].astype(F32) + from_r[j, 0].astype(F32)).astype(BF16)
        remote(buf.at[j, pl.ds(2 * prv, 2)], from_r.at[j, pl.ds(1, 2)], sems.at[j, 0], sems.at[j, 4], left)

    def ring_end(j, buf, from_l, from_r, me, sems):
        arrived(from_l.at[j, pl.ds(1, 2)], sems.at[j, 3])
        arrived(from_r.at[j, pl.ds(1, 2)], sems.at[j, 4])
        return [
            (buf[j, 2 * me + t].astype(F32) + from_l[j, 1 + t].astype(F32) + from_r[j, 1 + t].astype(F32)).astype(BF16)
            for t in range(2)
        ]

    ring_y = (part, part_l, part_r)
    ring_q = (quar, quar_l, quar_r)
    dev_y = (y, y_right, y_left)
    dev_q = (z_hi, at(z_hi_=turn(z_hi, 1)), at(z_hi_=turn(z_hi, 3)))

    def y_start(j):
        ring_start(j, *ring_y, *dev_y, s_y)

    def y_turn(j):
        ring_turn(j, *ring_y, *dev_y, s_y)

    def y_end(j):
        for t, value in enumerate(ring_end(j, *ring_y, y, s_y)):
            for q in range(4):
                quar[j, 4 * t + q] = value[q * 64:(q + 1) * 64]
        ring_start(j, *ring_q, *dev_q, s_q)

    def q_turn(j):
        ring_turn(j, *ring_q, *dev_q, s_q)

    def q_end(u):
        for t, value in enumerate(ring_end(u, *ring_q, z_hi, s_q)):
            res[u, pl.ds(64 * t, 64)] = value
        if u % 2:
            remote(res.at[u], cross.at[u // 2], s_cross.at[u // 2, 0], s_cross.at[u // 2, 1], sibling)

    later[0].wait()
    remote(tile[0], tile[1], s_tile.at[0], s_tile.at[1], sibling)
    arrived(plan_in, s_plan.at[1])
    to_scalars = pltpu.make_async_copy(plan_in, plan_s, s_local.at[NC + 3])
    to_scalars.start()
    gather_z(0)
    gather_start(1)
    gather_x(0)
    spread_own(1)
    gather_end(0)
    gather_z(1)
    multiply(0)
    y_start(0)
    to_scalars.wait()
    arrived(tile[1], s_tile.at[1])
    multiply(1)
    y_start(1)
    gather_x(1, (0, 1))
    y_turn(0)
    y_turn(1)
    pl.semaphore_wait(s_far.at[0], 1)
    pl.semaphore_wait(s_far.at[1], 1)
    y_end(0)
    gather_x(1, (2, 3))
    y_end(1)
    gather_end(1)
    multiply(3)
    y_start(3)
    multiply(2)
    y_start(2)
    q_turn(0)
    y_turn(3)
    q_turn(1)
    y_turn(2)
    y_end(3)
    q_end(0)
    q_end(1)
    y_end(2)
    q_turn(3)
    q_turn(2)
    q_end(3)
    q_end(2)

    later[1].wait()
    later[2].wait()

    def rows_of(whose, j):
        return pl.ds(pl.multiple_of(whose * HALF + j * FC, FC), FC)

    kept = [res[2 * j] for j in range(NC)]
    preact = sum(jnp.dot(kept[j], wts[rows_of(core, j)], preferred_element_type=F32) for j in range(NC))
    for j in range(NC):
        arrived(cross.at[j], s_cross.at[j, 1])
    swapped = [cross[j] for j in range(NC)]
    preact = preact + sum(
        jnp.dot(swapped[j], wts[rows_of(other, j)], preferred_element_type=F32) for j in range(NC)
    )
    low = jnp.minimum(preact, 0.0)
    slope = jnp.exp(low)
    near = low * (1.0 + low * (0.5 + low * (1.0 / 6 + low * (1.0 / 24))))
    output[...] = jnp.where(preact > 0, preact, jnp.where(low > -0.03125, near, slope - 1.0)).astype(BF16)
    grad_pre = (cot[...].astype(F32) * slope).astype(BF16)

    def term(aggregated):
        return scale * lax.dot_general(
            aggregated, grad_pre, (((0,), (0,)), ((), ())), preferred_element_type=F32
        )

    span = FC // 16
    for j in range(NC):
        value = term(swapped[j]).astype(BF16)
        for g in range(4):
            core_out[pl.ds(j * span, span), g] = value[:, g * 128:(g + 1) * 128].reshape(span, 16, 128)
    remote(core_out, core_in, s_gsend.at[0], s_grecv.at[0], sibling)
    for j in range(NC):
        value = term(kept[j])
        for g in range(4):
            mine[pl.ds(j * span, span), g] = value[:, g * 128:(g + 1) * 128].reshape(span, 16, 128)
    arrived(core_in, s_grecv.at[0])
    half[...] = (mine[...] + core_in[...].astype(F32)).astype(BF16)

    hops = (0, 1, 2, 1)
    far_first = sorted(((dx, dy) for dx in range(4) for dy in range(4)), key=lambda d: -hops[d[0]] - hops[d[1]])[:15]
    for dx, dy in far_first:
        i = turn(x, dx) * 4 + turn(y, dy)
        remote(half.at[i], xy_in.at[chip_xy], s_gsend.at[1], s_grecv.at[1], at_xy(i))
    xy_in[chip_xy] = half[chip_xy]
    arrived(xy_in.at[pl.ds(0, 15)], s_grecv.at[1])
    total = xy_in[0].astype(F32)
    for i in range(1, 16):
        total = total + xy_in[i].astype(F32)
    z_out[...] = total.astype(BF16)

    for d in (8, 7, 9, 6, 10, 5, 11, 4, 12, 3, 13, 2, 14, 1, 15):
        i = lax.rem(z + d, 16)
        remote(z_out.at[lax.rem(i, 4)], z_in.at[z], s_gsend.at[2], s_grecv.at[2], at_z(i))
    z_in[z] = z_out[z_lo]
    arrived(z_in.at[pl.ds(0, 15)], s_grecv.at[2])
    total = z_in[0].astype(F32)
    for i in range(1, 16):
        total = total + z_in[i].astype(F32)
    z_all[z_lo] = total.astype(BF16)
    for d in (2, 3, 1):
        remote(z_all.at[z_lo], z_all.at[z_lo], s_gsend.at[4], s_grecv.at[4], at(z_lo_=turn(z_lo, d)))
    arrived(z_all.at[pl.ds(0, 3)], s_grecv.at[4])
    full[core, chip_xy] = z_all[...]
    piece = full.at[core, chip_xy]
    for dx, dy in far_first:
        remote(piece, piece, s_gsend.at[5], s_grecv.at[5], at(x_=turn(x, dx), y_=turn(y, dy)))
    arrived(full.at[core, pl.ds(0, 15)], s_grecv.at[5])
    remote(full.at[core], full.at[core], s_gsend.at[6], s_grecv.at[6], sibling)

    def finish(whose):
        for g in range(4):
            weight_grad[pl.ds(pl.multiple_of(whose * 256, 256), 256), pl.ds(g * 128, 128)] = (
                full[whose, :, g].reshape(256, 128).astype(F32)
            )

    finish(core)
    arrived(full.at[other], s_grecv.at[6])
    finish(other)

    arrived(plan_out, s_plan.at[0])
    arrived(tile[0], s_tile.at[0])
    for j in range(NC):
        arrived(got[j].at[block, core], s_plan.at[2 + j])
        arrived(got[j].at[pl.ds(0, 15)], s_send.at[j])
        for u in (2 * j, 2 * j + 1):
            arrived(part.at[u, pl.ds(0, 6)], s_y.at[u, 0])
            arrived(quar.at[u, pl.ds(0, 6)], s_q.at[u, 0])
        arrived(cross.at[j], s_cross.at[j, 0])
    arrived(core_out, s_gsend.at[0])
    arrived(half.at[pl.ds(0, 15)], s_gsend.at[1])
    arrived(z_in.at[pl.ds(0, 15)], s_gsend.at[2])
    arrived(z_all.at[pl.ds(0, 3)], s_gsend.at[4])
    arrived(full.at[core, pl.ds(0, 15)], s_gsend.at[5])
    arrived(full.at[core], s_gsend.at[6])


def solution(mesh):
    vmem, smem, hbm = pltpu.VMEM, pltpu.SMEM, pltpu.HBM
    dma = pltpu.SemaphoreType.DMA

    def local(*operands):
        scale = 1.0 / math.sqrt(RBG * BLK * mesh.shape["row"])
        return pl.pallas_call(
            functools.partial(kernel, scale),
            out_shape=(
                jax.ShapeDtypeStruct((OWN, F), BF16),
                jax.ShapeDtypeStruct((F, F), F32),
            ),
            in_specs=[pl.BlockSpec(memory_space=s) for s in (hbm, hbm, hbm, smem, hbm, hbm)],
            out_specs=[pl.BlockSpec(memory_space=vmem)] * 2,
            scratch_shapes=[
                vmem((OWN, F), BF16),
                vmem((NC, OWN, FC), BF16),
                [vmem((CBG, 2, OWN, FC), BF16)] * NC,
                [vmem((KMAX, BLK, BLK), BF16)] * 2,
                vmem((F, F), BF16),
                vmem((OWN, F), BF16),
                vmem((8, 128), jnp.int32),
                vmem((8, 128), jnp.int32),
                smem((8, 128), jnp.int32),
                vmem((KMAX + 1, BLK, FC), BF16),
                vmem((2 * NC, RBG, BLK, FC), BF16),
                vmem((2 * NC, 3, BLK, FC), BF16),
                vmem((2 * NC, 3, BLK, FC), BF16),
                vmem((2 * NC, 8, 64, FC), BF16),
                vmem((2 * NC, 3, 64, FC), BF16),
                vmem((2 * NC, 3, 64, FC), BF16),
                vmem((2 * NC, OWN, FC), BF16),
                vmem((NC, OWN, FC), BF16),
                vmem((16, 4, 16, 128), F32),
                vmem((16, 4, 16, 128), BF16),
                vmem((16, 4, 16, 128), BF16),
                vmem((16, 4, 16, 128), BF16),
                vmem((16, 4, 16, 128), BF16),
                vmem((4, 16, 128), BF16),
                vmem((16, 16, 128), BF16),
                vmem((4, 16, 128), BF16),
                vmem((2, 16, 4, 16, 128), BF16),
                dma((NC + 5,)), dma((2 + NC,)), dma((NC,)), dma((2,)),
                dma((NC, 4)), dma((NC, 4)), dma((NC, 4)), dma((NC, 4)), dma((NC, 4)),
                dma((NC,)),
                dma((2 * NC, 5)), dma((2 * NC, 5)), dma((NC, 2)),
                dma((7,)), dma((7,)),
                pltpu.SemaphoreType.REGULAR((2,)),
                smem((1, 1, KMAX), jnp.int32),
            ],
            compiler_params=pltpu.CompilerParams(
                collective_id=0, has_side_effects=True, vmem_limit_bytes=48 << 20
            ),
        )(*[
            a if i == 3 else pltpu.with_memory_space_constraint(a, pltpu.HBM)
            for i, a in enumerate(operands)
        ])

    placed = (
        P(("col", "row"), None),
        P("row", "col", None, None, None),
        P("row", "col", None),
        P("row", "col"),
        P(),
        P(("row", "col"), None),
    )
    return jax.shard_map(
        local, mesh=mesh, in_specs=placed, out_specs=(P(("row", "col"), None), P()), check_vma=False
    )
```
